256 devices in a mesh: row: 16 (over x, y_lo, core), col: 16 (over y_hi, z).
Axes of the slice: x: 4, y: 4 (y_hi: 2, y_lo: 2; y = y_hi * 2 + y_lo), z: 8, core: 2. Of those that a mesh axis runs over, the one named last changes fastest.
Arguments:
- alignment: float32 [128, 768, 64], P('col', 'row'), may hold values from -6 to 6
- pair_rep: float32 [768, 768, 128], P('row', 'col'), may hold values from -6 to 6
- seq_mask: int32 [128], P('col'), may hold values 0 or 1
- res_mask: int32 [768], P('row'), may hold values 0 or 1
- left_weight: float32 [64, 32], replicated, may hold values from -0.75 to 0.75
- right_weight: float32 [64, 32], replicated, may hold values from -0.75 to 0.75
- w_outer: float32 [1024, 128], replicated, may hold values from -4 to 4
- w_logits: float32 [128, 8], replicated, may hold values from -45 to 45
- value_weight: float32 [64, 256], replicated, may hold values from -0.75 to 0.75
- gate_weight: float32 [64, 256], replicated, may hold values from -0.75 to 0.75
- output_weight: float32 [256, 64], replicated, may hold values from -6 to 6
Outputs:
- alignment_out: float32 [128, 768, 64], P('col', 'row')
- pair_out: float32 [768, 768, 128], P('row', 'col')
The draws below stay inside these ranges and needn't reach their ends.
All inputs are finite; a program needn't handle non-finite values. No bound on the sum of `seq_mask` or of `res_mask` on one device may be relied on, other than what follows from the above.
Results may differ from the reference program's by a relative error of at most 0.0003.
Values sent between devices are 32-bit elements; how exact they have to be, the bound alone decides.
No kernel may reach another device: no remote copies, remote signals or barrier semaphores. Data moves between devices by JAX's collectives and lax.ppermute only.
A program may use at most 128 MiB of HBM per device.

```python
import jax
import jax.numpy as jnp
from jax import lax

ALIGNED_WIDTH = 64
FACTOR_WIDTH = 32
PAIR_W = 128
AVERAGE_HEADS = 8
HEAD_CHANNELS = 32
RES_DEV = 48
SEQUENCE_COUNT = 128
RESIDUE_COUNT = 768
OUTER = 1024
N_ROW = 16


def draw_w_logits(key, part):
    first_key, second_key = jax.random.split(jax.random.fold_in(key, 11))
    normal_part = jnp.clip(jax.random.normal(first_key, (PAIR_W, AVERAGE_HEADS), jnp.float32), -5.0, 5.0)
    base = normal_part / PAIR_W ** 0.5
    levels = jnp.exp(jnp.linspace(jnp.log(0.5), jnp.log(2.0), AVERAGE_HEADS))
    shuffled = jax.random.permutation(second_key, AVERAGE_HEADS)
    return base * levels[shuffled][None, :]


def plant(array, key, smallest, top_value):
    extent = array.shape
    index_at = [jax.random.randint(jax.random.fold_in(key, axis), (), 0, extent[axis]) for axis in range(len(extent))]
    array = array.at[tuple(index_at)].set(smallest)
    longest = extent.index(max(extent))
    index_at[longest] = (index_at[longest] + 1) % extent[longest]
    return array.at[tuple(index_at)].set(top_value)


def level_of(stream_key, shape, cuts, low, largest):
    level = 1.0
    for position, parts in cuts:
        steps = jax.random.uniform(jax.random.fold_in(jax.random.fold_in(stream_key, 6), position), (parts,), jnp.float32, low / len(cuts), largest / len(cuts))
        level = level * jnp.repeat(jnp.exp(steps), shape[position] // parts).reshape((-1,) + (1,) * (len(shape) - 1 - position))
    return level


def gaussian(rng, dims, width, bound, pieces=(), dtype=jnp.bfloat16):
    result = width * jax.random.normal(rng, dims, jnp.float32)
    if pieces:
        result = result * level_of(rng, dims, pieces, -0.22, 0.18)
    return jnp.clip(result, -bound, bound).astype(dtype)


def setup_inputs(seed: int = 0) -> dict:
    arg_keys = jax.random.split(jax.random.key(seed), 12)
    alignment = gaussian(arg_keys[0], (SEQUENCE_COUNT, RESIDUE_COUNT, ALIGNED_WIDTH), 1.0, 6.0, ((0, 16), (1, 16)), jnp.float32)
    pair_rep = gaussian(arg_keys[1], (RESIDUE_COUNT, RESIDUE_COUNT, PAIR_W), 1.0, 6.0, ((0, 16), (1, 16)), jnp.float32)
    seq_mask = plant((jax.random.randint(arg_keys[2], (SEQUENCE_COUNT,), 0, 8) < 7).astype(jnp.int32), jax.random.fold_in(arg_keys[2], 1), 0, 1)
    res_mask = plant((jax.random.randint(arg_keys[3], (RESIDUE_COUNT,), 0, 8) < 7).astype(jnp.int32), jax.random.fold_in(arg_keys[3], 1), 0, 1)
    left_weight = gaussian(arg_keys[4], (ALIGNED_WIDTH, FACTOR_WIDTH), ALIGNED_WIDTH ** -0.5, 0.75, (), jnp.float32)
    right_weight = gaussian(arg_keys[5], (ALIGNED_WIDTH, FACTOR_WIDTH), ALIGNED_WIDTH ** -0.5, 0.75, (), jnp.float32)
    w_outer = gaussian(arg_keys[6], (OUTER, PAIR_W), 0.3, 4.0, (), jnp.float32)
    w_logits = draw_w_logits(jax.random.fold_in(arg_keys[11], 71), 0)
    value_weight = gaussian(arg_keys[8], (ALIGNED_WIDTH, AVERAGE_HEADS * HEAD_CHANNELS), ALIGNED_WIDTH ** -0.5, 0.75, (), jnp.float32)
    gate_weight = gaussian(arg_keys[9], (ALIGNED_WIDTH, AVERAGE_HEADS * HEAD_CHANNELS), ALIGNED_WIDTH ** -0.5, 0.75, (), jnp.float32)
    output_weight = gaussian(arg_keys[10], (AVERAGE_HEADS * HEAD_CHANNELS, ALIGNED_WIDTH), 0.5, 6.0, (), jnp.float32)
    return {"alignment": alignment, "pair_rep": pair_rep, "seq_mask": seq_mask, "res_mask": res_mask, "left_weight": left_weight, "right_weight": right_weight, "w_outer": w_outer, "w_logits": w_logits, "value_weight": value_weight, "gate_weight": gate_weight, "output_weight": output_weight}


epsilon = 1e-05
highest = lax.Precision.HIGHEST

def layer_norm(values):
    center = lax.optimization_barrier(jnp.mean(values, axis=-1, keepdims=True))
    centred = values - center
    return centred * lax.rsqrt(lax.optimization_barrier(jnp.mean(centred * centred, axis=-1, keepdims=True)) + epsilon)

def project(values, weight):
    return jnp.einsum('...c,cv->...v', values, weight, precision=highest)

def outer_block(left_rows, right_rows, w_outer):
    outer = jnp.einsum('sia,sjb->ijab', left_rows, right_rows, precision=highest)
    flat = outer.reshape(outer.shape[0] * outer.shape[1], outer.shape[2] * outer.shape[3])
    mapped = jnp.dot(flat, w_outer, precision=highest, preferred_element_type=jnp.float32)
    return mapped.reshape(outer.shape[0], outer.shape[1], w_outer.shape[1])

def reference(alignment, pair_rep, seq_mask, res_mask, left_weight, right_weight, w_outer, w_logits, value_weight, gate_weight, output_weight):
    normed = layer_norm(alignment)
    seq_live = seq_mask.astype(jnp.float32)
    res_live = res_mask.astype(jnp.float32)
    live = (seq_live[:, None] * res_live[None, :])[:, :, None]
    left_proj = project(normed, left_weight) * live
    right_proj = project(normed, right_weight) * live
    left_blocks = left_proj.reshape(SEQUENCE_COUNT, N_ROW, RES_DEV, FACTOR_WIDTH).transpose(1, 0, 2, 3)
    outer_sums = lax.map(lambda row_block: outer_block(row_block, right_proj, w_outer), left_blocks)
    outer_sums = outer_sums.reshape(RESIDUE_COUNT, RESIDUE_COUNT, PAIR_W)
    pair_count = jnp.maximum(res_live[:, None] * res_live[None, :] * jnp.sum(seq_live), 1.0)
    pair_out = pair_rep + outer_sums / pair_count[:, :, None]
    pair_normed = layer_norm(pair_out)
    logits = jnp.einsum('ijz,zh->hij', pair_normed, w_logits, precision=highest)
    logits = logits + ((res_live - 1.0) * 1000000000.0)[None, None, :]
    row_max = lax.optimization_barrier(jnp.max(logits, axis=2, keepdims=True))
    expo_terms = jnp.exp(logits - row_max)
    weights = expo_terms / lax.optimization_barrier(jnp.sum(expo_terms, axis=2, keepdims=True))
    values = project(normed, value_weight).reshape(SEQUENCE_COUNT, RESIDUE_COUNT, AVERAGE_HEADS, HEAD_CHANNELS)
    averaged = jnp.einsum('hij,sjhv->sihv', weights, values, precision=highest)
    averaged = averaged.reshape(SEQUENCE_COUNT, RESIDUE_COUNT, AVERAGE_HEADS * HEAD_CHANNELS)
    gate_open = jax.nn.sigmoid(project(normed, gate_weight))
    alignment_out = alignment + project(gate_open * averaged, output_weight)
    return (alignment_out, pair_out)
```

```python
import functools

import jax
import jax.numpy as jnp
from jax import lax
from jax.experimental import pallas as pl
from jax.experimental.pallas import tpu as pltpu
from jax.sharding import PartitionSpec as P

epsilon = 1e-05
highest = lax.Precision.HIGHEST
f32 = jnp.float32
bf16 = jnp.bfloat16
LANES = 128
Z_CHIPS = 8
ROWS_PER_STEP = 16


def split_two(values):
    high = values.astype(bf16)
    low = (values - high.astype(f32)).astype(bf16)
    return high, low


def mxu(left, right):
    return jnp.dot(left, right, preferred_element_type=f32)


def lane_group(shape, width):
    return lax.broadcasted_iota(jnp.int32, shape, len(shape) - 1) // width


def swap_groups(parts):
    group = lane_group(parts[0].shape, 32)
    upper = group >= 2
    odd = (group % 2) == 1
    first = list(parts)
    for v in (0, 1):
        mixed = pltpu.roll(jnp.where(upper, parts[v], parts[v + 2]), 64, 1)
        first[v] = jnp.where(upper, mixed, parts[v])
        first[v + 2] = jnp.where(upper, parts[v + 2], mixed)
    second = list(first)
    for v in (0, 2):
        second[v] = jnp.where(odd, pltpu.roll(first[v + 1], 32, 1), first[v])
        second[v + 1] = jnp.where(odd, first[v + 1], pltpu.roll(first[v], 96, 1))
    return second


def first_kernel(seq_ref, res_ref, align_ref, weight_ref, left_ref, right_ref, normed_ref, flat_ref, proj):
    seqs, residues, width = align_ref.shape
    values = align_ref[...].reshape(seqs * residues, width)
    center = jnp.mean(values, axis=-1, keepdims=True)
    centred = values - center
    normed = centred * lax.rsqrt(jnp.mean(centred * centred, axis=-1, keepdims=True) + epsilon)
    flat_ref[...] = normed
    for s in range(seqs):
        normed_ref[:, s * width : (s + 1) * width] = normed[s * residues : (s + 1) * residues]
    wide = jnp.dot(normed, weight_ref[...], precision=highest, preferred_element_type=f32)
    proj[0] = wide[:, :LANES]
    proj[1] = wide[:, LANES:]
    lane = lax.broadcasted_iota(jnp.int32, (seqs, LANES), 1)
    sub = lax.broadcasted_iota(jnp.int32, (seqs, LANES), 0)
    seq_live = jnp.zeros((seqs, LANES), f32)
    for s in range(seqs):
        seq_live = jnp.where(sub == s, seq_ref[s].astype(f32), seq_live)
    extra = jnp.where(lane == 64, seq_live, 0.0)
    group = lane // 32
    for quad in range(residues // 4):
        left = jnp.zeros((seqs, LANES), f32)
        right = jnp.zeros((seqs, LANES), f32)
        for g in range(4):
            i = quad * 4 + g
            live = res_ref[i].astype(f32)
            extra = jnp.where(lane == i, live, extra)
            here = group == g
            left = jnp.where(here, proj[0, pl.ds(i, seqs, stride=residues), :] * live, left)
            right = jnp.where(here, proj[1, pl.ds(i, seqs, stride=residues), :] * live, right)
        left_ref[:, quad * LANES : (quad + 1) * LANES] = left * seq_live
        right_ref[:, quad * LANES : (quad + 1) * LANES] = right * seq_live
    right_ref[:, residues * 32 :] = extra


def weights_kernel(outer_ref, value_ref, out_weight_ref, mapped_ref, mixed_ref, out_ref, tall):
    tall[...] = outer_ref[...]
    for b in range(32):
        high, low = split_two(tall[pl.ds(b, 32, stride=32), :])
        mapped_ref[b * 32 : (b + 1) * 32, :LANES] = high
        mapped_ref[b * 32 : (b + 1) * 32, LANES:] = low
    heads = mixed_ref.shape[0]
    values = value_ref[...]
    entry = lax.broadcasted_iota(jnp.int32, (256, LANES), 0)
    group = lane_group((256, LANES), 32)
    within = lax.broadcasted_iota(jnp.int32, (256, LANES), 1) % 32
    for h in range(heads):
        pick = jnp.where(entry == h * 32 + within, 1.0, 0.0)
        tiled = jnp.dot(values, pick, precision=highest, preferred_element_type=f32)
        four = jnp.concatenate([tiled] * 4, axis=0)
        block = jnp.where(entry // 64 == group, four, 0.0)
        high, low = split_two(block)
        mixed_ref[h, :, :LANES] = high
        mixed_ref[h, :, LANES:] = low
    high, low = split_two(out_weight_ref[...])
    out_ref[0] = high
    out_ref[1] = low


def outer_kernel(res_ref, left_ref, right_ref, mapped_ref, pair_ref, head_ref, pair_out_ref, logits_ref, tall, right_two, outer, high_ref, low_ref, seen):
    step = pl.program_id(0)
    cols = 48

    @pl.when(step == 0)
    def _():
        tall[...] = right_ref[:, : cols * 32].T
        for b in range(32):
            high, low = split_two(tall[pl.ds(b, cols, stride=32), :])
            right_two[b * cols : (b + 1) * cols, :LANES] = high
            right_two[b * cols : (b + 1) * cols, LANES:] = low
        extra = right_ref[:, cols * 32 :]
        lane = lax.broadcasted_iota(jnp.int32, (LANES, LANES), 1)
        total = jnp.sum(jnp.where(lane == 64, extra, 0.0))
        live_cols = extra.T[:cols, :1]
        seen[0] = jnp.broadcast_to(live_cols * total, (cols, LANES))
        seen[1] = jnp.broadcast_to((live_cols - 1.0) * 1e9, (cols, LANES))

    left_high, left_low = split_two(left_ref[...])
    both = right_two[...]
    outer[...] = mxu(both, jnp.concatenate([left_high, left_high], axis=0)) + mxu(both[:, :LANES], left_low)
    for quad in range(ROWS_PER_STEP // 4):
        for four in range(8):
            parts = [
                outer[(four * 4 + v) * cols : (four * 4 + v + 1) * cols, quad * LANES : (quad + 1) * LANES]
                for v in range(4)
            ]
            for g, part in enumerate(swap_groups(parts)):
                high, low = split_two(part)
                at = (quad * 4 + g) * cols
                high_ref[at : at + cols, four * LANES : (four + 1) * LANES] = high
                low_ref[at : at + cols, four * LANES : (four + 1) * LANES] = low
    wide = mxu(high_ref[...], mapped_ref[...])
    sums = wide[:, :LANES] + wide[:, LANES:] + mxu(low_ref[...], mapped_ref[:, :LANES])
    head_high, head_low = split_two(head_ref[...])
    head_high = jnp.concatenate([head_high, head_high], axis=0)
    head_low = jnp.concatenate([head_low, head_low], axis=0)
    pairs = []
    for i in range(ROWS_PER_STEP):
        live = res_ref[step * ROWS_PER_STEP + i].astype(f32)
        count = jnp.maximum(seen[0] * live, 1.0)
        pair = pair_ref[i] + sums[i * cols : (i + 1) * cols] / count
        pair_out_ref[i] = pair
        pairs.append(pair)
    pair = jnp.concatenate(pairs, axis=0)
    centred = pair - jnp.mean(pair, axis=-1, keepdims=True)
    normed = centred * lax.rsqrt(jnp.mean(centred * centred, axis=-1, keepdims=True) + epsilon)
    high, low = split_two(normed)
    normed_two = jnp.concatenate([high, low], axis=1)
    logits = mxu(normed_two, head_high) + mxu(normed_two, head_low)
    lane = lax.broadcasted_iota(jnp.int32, (cols, LANES), 1)
    line = jnp.zeros((cols, LANES), f32)
    for i in range(ROWS_PER_STEP):
        line = jnp.where(lane // 8 == i, pltpu.roll(logits[i * cols : (i + 1) * cols], 8 * i, 1) if i else logits[:cols], line)
    logits_ref[...] = line + seen[1]


def middle_kernel(align_normed_ref, normed_ref, gate_ref, turned_high_ref, turned_low_ref, open_ref):
    high, low = split_two(normed_ref[...].T)
    turned_high_ref[...] = high
    turned_low_ref[...] = low
    wide = jnp.dot(align_normed_ref[...], gate_ref[...], precision=highest, preferred_element_type=f32)
    open_ref[...] = jax.nn.sigmoid(wide)


def last_kernel(*refs):
    pieces_in = refs[:Z_CHIPS]
    turned_high_ref, turned_low_ref, mixed_ref, open_ref, out_weight_ref, align_ref, out_ref, held, averaged = refs[Z_CHIPS:]
    heads = mixed_ref.shape[0]
    rows = 48
    me = lax.axis_index("col")
    side, place = me // Z_CHIPS, me % Z_CHIPS
    for k, piece in enumerate(pieces_in):
        at = lax.rem(place + k, Z_CHIPS) * rows
        for other in range(2):
            half = side if other == 0 else 1 - side
            start = pl.multiple_of(half * (Z_CHIPS * rows) + at, 8)
            held[pl.ds(start, rows), :] = piece[other]
    logits = held[...]
    top = jnp.max(logits, axis=0, keepdims=True)
    expo = jnp.exp(logits - top)
    total = jnp.sum(expo, axis=0, keepdims=True)
    high, low = split_two(expo)
    turned_high = turned_high_ref[...]
    summed = mxu(turned_high, high) + mxu(turned_high, low) + mxu(turned_low_ref[...], high)
    turned = (summed / total).T
    for k in range(4):
        averaged[k] = turned[:, k * LANES : (k + 1) * LANES]
    ready = []
    for h in range(heads):
        one = [averaged[k, pl.ds(h, rows, stride=heads), :] for k in range(4)]
        one = jnp.concatenate([jnp.concatenate(one[:2], axis=1), jnp.concatenate(one[2:], axis=1)], axis=0)
        high, low = split_two(one)
        wide = mxu(high, mixed_ref[h])
        ready.append(wide[:, :LANES] + wide[:, LANES:] + mxu(low, mixed_ref[h, :, :LANES]))
    pieces = [[None, None] for _ in range(8)]
    for half in range(2):
        for s, part in enumerate(swap_groups(ready[half * 4 : half * 4 + 4])):
            pieces[s][half] = part[:rows]
            pieces[s + 4][half] = part[rows:]
    merged = jnp.concatenate([jnp.concatenate(p, axis=1) for p in pieces], axis=0)
    high, low = split_two(open_ref[...] * merged)
    result = mxu(high, out_weight_ref[0]) + mxu(high, out_weight_ref[1]) + mxu(low, out_weight_ref[0])
    out_ref[...] = align_ref[...] + result.reshape(out_ref.shape)


def spread(shard, axis):
    devices = lax.axis_size(axis)
    return lax.all_to_all(jnp.broadcast_to(shard[None], (devices, *shard.shape)), axis, 0, 0, tiled=True)


def ring_pieces(shard, axis):
    devices = lax.axis_size(axis)
    ring = Z_CHIPS
    other = lax.ppermute(shard, axis, [(d, (d + ring) % devices) for d in range(devices)])
    ahead = [(d, d // ring * ring + (d + 1) % ring) for d in range(devices)]
    back = [(d, d // ring * ring + (d + ring - 1) % ring) for d in range(devices)]
    pieces = [None] * ring
    pieces[0] = up = down = jnp.stack([shard, other])
    for hop in range(1, ring // 2 + 1):
        up = lax.ppermute(up, axis, ahead)
        pieces[ring - hop] = up
        if hop < ring // 2:
            down = lax.ppermute(down, axis, back)
            pieces[hop] = down
    return pieces


def call(kernel, outs, scratch=(), **more):
    return pl.pallas_call(
        kernel,
        out_shape=outs,
        scratch_shapes=scratch,
        compiler_params=pltpu.CompilerParams(vmem_limit_bytes=48 * 1024 * 1024),
        **more,
    )


def shape(dims, dtype=f32):
    return jax.ShapeDtypeStruct(dims, dtype)


VMEM = pl.BlockSpec(memory_space=pltpu.VMEM)
SMEM = pl.BlockSpec(memory_space=pltpu.SMEM)


def per_device(n_row, n_col, alignment, pair_rep, seq_mask, res_mask, left_weight, right_weight, w_outer, w_logits, value_weight, gate_weight, output_weight):
    seqs, rows, width = alignment.shape
    cols = pair_rep.shape[1]
    pair_width = pair_rep.shape[2]
    four_weights = jnp.concatenate([left_weight] * 4 + [right_weight] * 4, axis=1)
    left, right, normed, normed_flat = call(
        first_kernel,
        (shape((seqs, rows * 32)), shape((seqs, rows * 32 + LANES)), shape((rows, seqs * width)), shape((seqs * rows, width))),
        scratch=[pltpu.VMEM((2, seqs * rows, LANES), f32)],
        in_specs=[SMEM, SMEM, VMEM, VMEM],
    )(seq_mask, res_mask, alignment, four_weights)
    turn = [(r * n_col + c, c * n_col + r) for r in range(n_row) for c in range(n_col)]
    right_here = lax.ppermute(right, ("row", "col"), turn)
    right_all = spread(right_here, "row").reshape(n_row * seqs, -1)
    left_all = spread(left, "col").reshape(n_col * seqs, -1)
    mapped, mixed, out_two = call(
        weights_kernel,
        (shape((1024, 256), bf16), shape((8, 256, 256), bf16), shape((2, 256, 64), bf16)),
        scratch=[pltpu.VMEM((1024, LANES), f32)],
    )(w_outer, value_weight, output_weight)
    head_pad = jnp.pad(w_logits, ((0, 0), (0, LANES - w_logits.shape[1])))
    steps = rows // ROWS_PER_STEP
    pair_out, logits = pl.pallas_call(
        outer_kernel,
        grid=(steps,),
        out_shape=(shape(pair_rep.shape), shape((cols, steps * LANES))),
        in_specs=[
            SMEM,
            pl.BlockSpec((n_col * seqs, ROWS_PER_STEP * 32), lambda t: (0, t)),
            pl.BlockSpec(right_all.shape, lambda t: (0, 0)),
            pl.BlockSpec((1024, 256), lambda t: (0, 0)),
            pl.BlockSpec((ROWS_PER_STEP, cols, pair_width), lambda t: (t, 0, 0)),
            pl.BlockSpec((pair_width, LANES), lambda t: (0, 0)),
        ],
        out_specs=[
            pl.BlockSpec((ROWS_PER_STEP, cols, pair_width), lambda t: (t, 0, 0)),
            pl.BlockSpec((cols, LANES), lambda t: (0, t)),
        ],
        scratch_shapes=[
            pltpu.VMEM((cols * 32, LANES), f32),
            pltpu.VMEM((cols * 32, 256), bf16),
            pltpu.VMEM((cols * 32, ROWS_PER_STEP * 32), f32),
            pltpu.VMEM((ROWS_PER_STEP * cols, 1024), bf16),
            pltpu.VMEM((ROWS_PER_STEP * cols, 1024), bf16),
            pltpu.VMEM((2, cols, LANES), f32),
        ],
        compiler_params=pltpu.CompilerParams(vmem_limit_bytes=48 * 1024 * 1024),
    )(res_mask, left_all, right_all, mapped, pair_rep, head_pad)
    normed_all = lax.all_gather(normed, "row", axis=0, tiled=True)
    turned_high, turned_low, opened = call(
        middle_kernel,
        (shape((seqs * width, n_row * rows), bf16), shape((seqs * width, n_row * rows), bf16), shape((seqs * rows, gate_weight.shape[1]))),
    )(normed_flat, normed_all, gate_weight)
    pieces = ring_pieces(logits, "col")
    alignment_out = call(
        last_kernel,
        shape(alignment.shape),
        scratch=[pltpu.VMEM((n_row * rows, steps * LANES), f32), pltpu.VMEM((4, steps * LANES, LANES), f32)],
    )(*pieces, turned_high, turned_low, mixed, opened, out_two, alignment)
    return alignment_out, pair_out


def solution(mesh):
    in_specs = (
        P("col", "row", None),
        P("row", "col", None),
        P("col"),
        P("row"),
        P(),
        P(),
        P(),
        P(),
        P(),
        P(),
        P(),
    )
    out_specs = (P("col", "row", None), P("row", "col", None))
    body = functools.partial(per_device, mesh.shape["row"], mesh.shape["col"])
    return jax.shard_map(body, mesh=mesh, in_specs=in_specs, out_specs=out_specs, check_vma=False)
```

```python
import functools

import jax
import jax.numpy as jnp
from jax import lax
from jax.experimental import pallas as pl
from jax.experimental.pallas import tpu as pltpu
from jax.sharding import PartitionSpec as P

epsilon = 1e-05
highest = lax.Precision.HIGHEST
f32 = jnp.float32
bf16 = jnp.bfloat16
LANES = 128
Z_CHIPS = 8
ROWS_PER_STEP = 16


def split_two(values):
    high = values.astype(bf16)
    low = (values - high.astype(f32)).astype(bf16)
    return high, low


def mxu(left, right):
    return jnp.dot(left, right, preferred_element_type=f32)


def lane_group(shape, width):
    return lax.broadcasted_iota(jnp.int32, shape, len(shape) - 1) // width


def swap_groups(parts):
    group = lane_group(parts[0].shape, 32)
    upper = group >= 2
    odd = (group % 2) == 1
    first = list(parts)
    for v in (0, 1):
        mixed = pltpu.roll(jnp.where(upper, parts[v], parts[v + 2]), 64, 1)
        first[v] = jnp.where(upper, mixed, parts[v])
        first[v + 2] = jnp.where(upper, parts[v + 2], mixed)
    second = list(first)
    for v in (0, 2):
        second[v] = jnp.where(odd, pltpu.roll(first[v + 1], 32, 1), first[v])
        second[v + 1] = jnp.where(odd, first[v + 1], pltpu.roll(first[v], 96, 1))
    return second


def first_kernel(seq_in, res_in, align_in, left_in, right_in, left_ref, right_ref, normed_ref, flat_ref, seq_ref, res_ref, align_ref, weight_ref, proj, sems):
    copies = [
        pltpu.make_async_copy(align_in, align_ref, sems.at[0]),
        pltpu.make_async_copy(left_in, weight_ref.at[0], sems.at[1]),
        pltpu.make_async_copy(right_in, weight_ref.at[1], sems.at[2]),
        pltpu.make_async_copy(seq_in, seq_ref, sems.at[3]),
        pltpu.make_async_copy(res_in, res_ref, sems.at[4]),
    ]
    for copy in copies:
        copy.start()
    for copy in copies:
        copy.wait()
    seqs, residues, width = align_ref.shape
    values = align_ref[...].reshape(seqs * residues, width)
    center = jnp.mean(values, axis=-1, keepdims=True)
    centred = values - center
    normed = centred * lax.rsqrt(jnp.mean(centred * centred, axis=-1, keepdims=True) + epsilon)
    flat_ref[...] = normed
    for s in range(seqs):
        normed_ref[:, s * width : (s + 1) * width] = normed[s * residues : (s + 1) * residues]
    weight = jnp.concatenate([weight_ref[0]] * 4 + [weight_ref[1]] * 4, axis=0)
    wide = lax.dot_general(normed, weight, (((1,), (1,)), ((), ())), precision=highest, preferred_element_type=f32)
    proj[0] = wide[:, :LANES]
    proj[1] = wide[:, LANES:]
    lane = lax.broadcasted_iota(jnp.int32, (seqs, LANES), 1)
    sub = lax.broadcasted_iota(jnp.int32, (seqs, LANES), 0)
    seq_live = jnp.zeros((seqs, LANES), f32)
    for s in range(seqs):
        seq_live = jnp.where(sub == s, seq_ref[s].astype(f32), seq_live)
    extra = jnp.where(lane == 64, seq_live, 0.0)
    group = lane // 32
    for quad in range(residues // 4):
        left = jnp.zeros((seqs, LANES), f32)
        right = jnp.zeros((seqs, LANES), f32)
        for g in range(4):
            i = quad * 4 + g
            live = res_ref[i].astype(f32)
            extra = jnp.where(lane == i, live, extra)
            here = group == g
            left = jnp.where(here, proj[0, pl.ds(i, seqs, stride=residues), :] * live, left)
            right = jnp.where(here, proj[1, pl.ds(i, seqs, stride=residues), :] * live, right)
        left_ref[:, quad * LANES : (quad + 1) * LANES] = left * seq_live
        right_ref[:, quad * LANES : (quad + 1) * LANES] = right * seq_live
    right_ref[:, residues * 32 :] = extra


def weights_kernel(outer_ref, value_ref, out_weight_ref, mapped_ref, mixed_ref, out_ref, tall):
    tall[...] = outer_ref[...]
    for b in range(32):
        high, low = split_two(tall[pl.ds(b, 32, stride=32), :])
        mapped_ref[b * 32 : (b + 1) * 32, :LANES] = high
        mapped_ref[b * 32 : (b + 1) * 32, LANES:] = low
    heads = mixed_ref.shape[0]
    values = value_ref[...]
    entry = lax.broadcasted_iota(jnp.int32, (256, LANES), 0)
    group = lane_group((256, LANES), 32)
    within = lax.broadcasted_iota(jnp.int32, (256, LANES), 1) % 32
    for h in range(heads):
        pick = jnp.where(entry == h * 32 + within, 1.0, 0.0)
        tiled = jnp.dot(values, pick, precision=highest, preferred_element_type=f32)
        four = jnp.concatenate([tiled] * 4, axis=0)
        block = jnp.where(entry // 64 == group, four, 0.0)
        high, low = split_two(block)
        mixed_ref[h, :, :LANES] = high
        mixed_ref[h, :, LANES:] = low
    high, low = split_two(out_weight_ref[...].T)
    out_ref[0] = high
    out_ref[1] = low


def outer_kernel(*refs):
    res_ref = refs[0]
    left_pieces = refs[1 : 1 + Z_CHIPS]
    right_pieces = refs[1 + Z_CHIPS : 9 + Z_CHIPS]
    mapped_ref, pair_ref, head_ref, pair_out_ref, logits_ref = refs[9 + Z_CHIPS : 14 + Z_CHIPS]
    left_all, right_ref, tall, right_two, outer, high_ref, low_ref, seen, heads_two = refs[14 + Z_CHIPS :]
    step = pl.program_id(0)
    cols = 48

    @pl.when(step == 0)
    def _():
        me = lax.axis_index("col")
        side, place = me // Z_CHIPS, lax.rem(me, Z_CHIPS)
        for k, piece in enumerate(left_pieces):
            at = lax.rem(place + k, Z_CHIPS)
            left_all[pl.ds(pl.multiple_of((side * Z_CHIPS + at) * 8, 8), 8), :] = piece[0]
            left_all[pl.ds(pl.multiple_of(((1 - side) * Z_CHIPS + at) * 8, 8), 8), :] = piece[1]
        row = lax.axis_index("row")
        x, y, core = row // 4, lax.rem(row // 2, 2), lax.rem(row, 2)
        for k, piece in enumerate(right_pieces):
            at = lax.rem(x + k % 4, 4) * 4 + (core if k < 4 else 1 - core)
            right_ref[pl.ds(pl.multiple_of((at + y * 2) * 8, 8), 8), :] = piece[0]
            right_ref[pl.ds(pl.multiple_of((at + (1 - y) * 2) * 8, 8), 8), :] = piece[1]
        tall[...] = right_ref[:, : cols * 32].T
        for b in range(32):
            high, low = split_two(tall[pl.ds(b, cols, stride=32), :])
            right_two[b * cols : (b + 1) * cols, :LANES] = high
            right_two[b * cols : (b + 1) * cols, LANES:] = low
        extra = right_ref[:, cols * 32 :]
        lane = lax.broadcasted_iota(jnp.int32, (LANES, LANES), 1)
        total = jnp.sum(jnp.where(lane == 64, extra, 0.0))
        live_cols = extra.T[:cols, :1]
        seen[0] = jnp.broadcast_to(live_cols * total, (cols, LANES))
        seen[1] = jnp.broadcast_to((live_cols - 1.0) * 1e9, (cols, LANES))
        head = jnp.concatenate([head_ref[...], jnp.zeros((LANES - head_ref.shape[0], LANES), f32)], axis=0).T
        head_high, head_low = split_two(head)
        heads_two[0, :LANES] = head_high
        heads_two[0, LANES:] = head_high
        heads_two[1, :LANES] = head_low
        heads_two[1, LANES:] = head_low

    left_high, left_low = split_two(left_all[:, pl.ds(pl.multiple_of(step * (ROWS_PER_STEP * 32), LANES), ROWS_PER_STEP * 32)])
    both = right_two[...]
    outer[...] = mxu(both, jnp.concatenate([left_high, left_high], axis=0)) + mxu(both[:, :LANES], left_low)
    for quad in range(ROWS_PER_STEP // 4):
        for four in range(8):
            parts = [
                outer[(four * 4 + v) * cols : (four * 4 + v + 1) * cols, quad * LANES : (quad + 1) * LANES]
                for v in range(4)
            ]
            for g, part in enumerate(swap_groups(parts)):
                high, low = split_two(part)
                at = (quad * 4 + g) * cols
                high_ref[at : at + cols, four * LANES : (four + 1) * LANES] = high
                low_ref[at : at + cols, four * LANES : (four + 1) * LANES] = low
    wide = mxu(high_ref[...], mapped_ref[...])
    sums = wide[:, :LANES] + wide[:, LANES:] + mxu(low_ref[...], mapped_ref[:, :LANES])
    pairs = []
    for i in range(ROWS_PER_STEP):
        live = res_ref[step * ROWS_PER_STEP + i].astype(f32)
        count = jnp.maximum(seen[0] * live, 1.0)
        pair = pair_ref[i] + sums[i * cols : (i + 1) * cols] / count
        pair_out_ref[i] = pair
        pairs.append(pair)
    pair = jnp.concatenate(pairs, axis=0)
    centred = pair - jnp.mean(pair, axis=-1, keepdims=True)
    normed = centred * lax.rsqrt(jnp.mean(centred * centred, axis=-1, keepdims=True) + epsilon)
    high, low = split_two(normed)
    normed_two = jnp.concatenate([high, low], axis=1)
    logits = mxu(normed_two, heads_two[0]) + mxu(normed_two, heads_two[1])
    lane = lax.broadcasted_iota(jnp.int32, (cols, LANES), 1)
    line = jnp.zeros((cols, LANES), f32)
    for i in range(ROWS_PER_STEP):
        line = jnp.where(lane // 8 == i, pltpu.roll(logits[i * cols : (i + 1) * cols], 8 * i, 1) if i else logits[:cols], line)
    logits_ref[...] = line + seen[1]


def middle_kernel(align_normed_ref, gate_ref, *refs):
    pieces = refs[:8]
    turned_high_ref, turned_low_ref, open_ref, held = refs[8:]
    residues = pieces[0].shape[1]
    row = lax.axis_index("row")
    x, y, core = row // 4, lax.rem(row // 2, 2), lax.rem(row, 2)
    for k, piece in enumerate(pieces):
        at = lax.rem(x + k % 4, 4) * 4 + (core if k < 4 else 1 - core)
        held[pl.ds(pl.multiple_of((at + y * 2) * residues, 8), residues), :] = piece[0]
        held[pl.ds(pl.multiple_of((at + (1 - y) * 2) * residues, 8), residues), :] = piece[1]
    high, low = split_two(held[...].T)
    turned_high_ref[...] = high
    turned_low_ref[...] = low
    wide = jnp.dot(align_normed_ref[...], gate_ref[...], precision=highest, preferred_element_type=f32)
    open_ref[...] = jax.nn.sigmoid(wide)


def last_kernel(*refs):
    pieces_in = refs[:Z_CHIPS]
    turned_high_ref, turned_low_ref, mixed_ref, open_ref, out_weight_ref, align_ref, out_ref, held, averaged = refs[Z_CHIPS:]
    heads = mixed_ref.shape[0]
    rows = 48
    me = lax.axis_index("col")
    side, place = me // Z_CHIPS, lax.rem(me, Z_CHIPS)
    for k, piece in enumerate(pieces_in):
        at = lax.rem(place + k, Z_CHIPS) * rows
        for other in range(2):
            half = side if other == 0 else 1 - side
            start = pl.multiple_of(half * (Z_CHIPS * rows) + at, 8)
            held[pl.ds(start, rows), :] = piece[other]
    logits = held[...]
    top = jnp.max(logits, axis=0, keepdims=True)
    expo = jnp.exp(logits - top)
    total = jnp.sum(expo, axis=0, keepdims=True)
    high, low = split_two(expo)
    turned_high = turned_high_ref[...]
    summed = mxu(turned_high, high) + mxu(turned_high, low) + mxu(turned_low_ref[...], high)
    turned = (summed / total).T
    for k in range(4):
        averaged[k] = turned[:, k * LANES : (k + 1) * LANES]
    ready = []
    for h in range(heads):
        one = [averaged[k, pl.ds(h, rows, stride=heads), :] for k in range(4)]
        one = jnp.concatenate([jnp.concatenate(one[:2], axis=1), jnp.concatenate(one[2:], axis=1)], axis=0)
        high, low = split_two(one)
        wide = mxu(high, mixed_ref[h])
        ready.append(wide[:, :LANES] + wide[:, LANES:] + mxu(low, mixed_ref[h, :, :LANES]))
    pieces = [[None, None] for _ in range(8)]
    for half in range(2):
        for s, part in enumerate(swap_groups(ready[half * 4 : half * 4 + 4])):
            pieces[s][half] = part[:rows]
            pieces[s + 4][half] = part[rows:]
    merged = jnp.concatenate([jnp.concatenate(p, axis=1) for p in pieces], axis=0)
    high, low = split_two(open_ref[...] * merged)
    result = mxu(high, out_weight_ref[0]) + mxu(high, out_weight_ref[1]) + mxu(low, out_weight_ref[0])
    out_ref[...] = align_ref[...] + result.reshape(out_ref.shape)


def row_pieces(shard, axis):
    devices = lax.axis_size(axis)
    both = jnp.stack([shard, lax.ppermute(shard, axis, [(d, d ^ 2) for d in range(devices)])])
    pieces = [both] + [
        lax.ppermute(both, axis, [(d, (d + devices - 4 * k) % devices) for d in range(devices)]) for k in (1, 2, 3)
    ]
    return pieces + [lax.ppermute(piece, axis, [(d, d ^ 1) for d in range(devices)]) for piece in pieces]


def ring_pieces(shard, axis):
    devices = lax.axis_size(axis)
    ring = Z_CHIPS
    other = lax.ppermute(shard, axis, [(d, (d + ring) % devices) for d in range(devices)])
    ahead = [(d, d // ring * ring + (d + 1) % ring) for d in range(devices)]
    back = [(d, d // ring * ring + (d + ring - 1) % ring) for d in range(devices)]
    pieces = [None] * ring
    pieces[0] = up = down = jnp.stack([shard, other])
    for hop in range(1, ring // 2 + 1):
        up = lax.ppermute(up, axis, ahead)
        pieces[ring - hop] = up
        if hop < ring // 2:
            down = lax.ppermute(down, axis, back)
            pieces[hop] = down
    return pieces


def call(kernel, outs, limit, scratch=(), **more):
    return pl.pallas_call(
        kernel,
        out_shape=outs,
        scratch_shapes=list(scratch),
        compiler_params=pltpu.CompilerParams(vmem_limit_bytes=limit * 1024 * 1024),
        **more,
    )


def shape(dims, dtype=f32):
    return jax.ShapeDtypeStruct(dims, dtype)


VMEM = pl.BlockSpec(memory_space=pltpu.VMEM)
HBM = pl.BlockSpec(memory_space=pltpu.HBM)
SMEM = pl.BlockSpec(memory_space=pltpu.SMEM)


def per_device(n_row, n_col, alignment, pair_rep, seq_mask, res_mask, left_weight, right_weight, w_outer, w_logits, value_weight, gate_weight, output_weight):
    seqs, rows, width = alignment.shape
    cols = pair_rep.shape[1]
    pair_width = pair_rep.shape[2]
    left, right, normed, normed_flat = call(
        first_kernel,
        (shape((seqs, rows * 32)), shape((seqs, rows * 32 + LANES)), shape((rows, seqs * width)), shape((seqs * rows, width))),
        8,
        scratch=[
            pltpu.SMEM(seq_mask.shape, jnp.int32),
            pltpu.SMEM(res_mask.shape, jnp.int32),
            pltpu.VMEM(alignment.shape, f32),
            pltpu.VMEM((2, 32, width), f32),
            pltpu.VMEM((2, seqs * rows, LANES), f32),
            pltpu.SemaphoreType.DMA((5,)),
        ],
        in_specs=[HBM] * 5,
    )(seq_mask, res_mask, alignment, left_weight.T, right_weight.T)
    turn = [(r * n_col + c, c * n_col + r) for r in range(n_row) for c in range(n_col)]
    right_here = lax.ppermute(right, ("row", "col"), turn)
    left_pieces = ring_pieces(left, "col")
    right_pieces = row_pieces(right_here, "row")
    mapped, mixed, out_two = call(
        weights_kernel,
        (shape((1024, 256), bf16), shape((8, 256, 256), bf16), shape((2, 256, 64), bf16)),
        12,
        scratch=[pltpu.VMEM((1024, LANES), f32)],
    )(w_outer, value_weight, output_weight.T)
    steps = rows // ROWS_PER_STEP
    whole = lambda dims: pl.BlockSpec(dims, lambda t: (0,) * len(dims))
    pair_out, logits = pl.pallas_call(
        outer_kernel,
        grid=(steps,),
        out_shape=(shape(pair_rep.shape), shape((cols, steps * LANES))),
        in_specs=[SMEM]
        + [whole(left_pieces[0].shape)] * 8
        + [whole(right_pieces[0].shape)] * 8
        + [
            whole((1024, 256)),
            pl.BlockSpec((ROWS_PER_STEP, cols, pair_width), lambda t: (t, 0, 0)),
            whole((8, LANES)),
        ],
        out_specs=[
            pl.BlockSpec((ROWS_PER_STEP, cols, pair_width), lambda t: (t, 0, 0)),
            pl.BlockSpec((cols, LANES), lambda t: (0, t)),
        ],
        scratch_shapes=[
            pltpu.VMEM((n_col * seqs, rows * 32), f32),
            pltpu.VMEM((n_row * seqs, rows * 32 + LANES), f32),
            pltpu.VMEM((cols * 32, LANES), f32),
            pltpu.VMEM((cols * 32, 256), bf16),
            pltpu.VMEM((cols * 32, ROWS_PER_STEP * 32), f32),
            pltpu.VMEM((ROWS_PER_STEP * cols, 1024), bf16),
            pltpu.VMEM((ROWS_PER_STEP * cols, 1024), bf16),
            pltpu.VMEM((2, cols, LANES), f32),
            pltpu.VMEM((2, 256, LANES), bf16),
        ],
        compiler_params=pltpu.CompilerParams(vmem_limit_bytes=32 * 1024 * 1024),
        cost_estimate=pl.CostEstimate(flops=10**10, bytes_accessed=10**7, transcendentals=0),
    )(res_mask, *left_pieces, *right_pieces, mapped, pair_rep, w_logits.T)
    normed_pieces = row_pieces(normed, "row")
    turned_high, turned_low, opened = call(
        middle_kernel,
        (shape((seqs * width, n_row * rows), bf16), shape((seqs * width, n_row * rows), bf16), shape((seqs * rows, gate_weight.shape[1]))),
        12,
        scratch=[pltpu.VMEM((n_row * rows, seqs * width), f32)],
    )(normed_flat, gate_weight, *normed_pieces)
    pieces = ring_pieces(logits, "col")
    alignment_out = call(
        last_kernel,
        shape(alignment.shape),
        24,
        scratch=[pltpu.VMEM((n_row * rows, steps * LANES), f32), pltpu.VMEM((4, steps * LANES, LANES), f32)],
    )(*pieces, turned_high, turned_low, mixed, opened, out_two, alignment)
    return alignment_out, pair_out


def solution(mesh):
    in_specs = (
        P("col", "row", None),
        P("row", "col", None),
        P("col"),
        P("row"),
        P(),
        P(),
        P(),
        P(),
        P(),
        P(),
        P(),
    )
    out_specs = (P("col", "row", None), P("row", "col", None))
    body = functools.partial(per_device, mesh.shape["row"], mesh.shape["col"])
    return jax.shard_map(body, mesh=mesh, in_specs=in_specs, out_specs=out_specs, check_vma=False)
```

```python
import functools

import jax
import jax.numpy as jnp
from jax import lax
from jax.experimental import pallas as pl
from jax.experimental.pallas import tpu as pltpu
from jax.sharding import PartitionSpec as P

epsilon = 1e-05
highest = lax.Precision.HIGHEST
f32 = jnp.float32
bf16 = jnp.bfloat16
LANES = 128
Z_CHIPS = 8
ROWS_PER_STEP = 16


def split_two(values):
    high = values.astype(bf16)
    low = (values - high.astype(f32)).astype(bf16)
    return high, low


def mxu(left, right):
    return jnp.dot(left, right, preferred_element_type=f32)


def lane_group(shape, width):
    return lax.broadcasted_iota(jnp.int32, shape, len(shape) - 1) // width


def swap_groups(parts):
    group = lane_group(parts[0].shape, 32)
    upper = group >= 2
    odd = (group % 2) == 1
    first = list(parts)
    for v in (0, 1):
        mixed = pltpu.roll(jnp.where(upper, parts[v], parts[v + 2]), 64, 1)
        first[v] = jnp.where(upper, mixed, parts[v])
        first[v + 2] = jnp.where(upper, parts[v + 2], mixed)
    second = list(first)
    for v in (0, 2):
        second[v] = jnp.where(odd, pltpu.roll(first[v + 1], 32, 1), first[v])
        second[v + 1] = jnp.where(odd, first[v + 1], pltpu.roll(first[v], 96, 1))
    return second


def copied(pairs, sems):
    copies = [pltpu.make_async_copy(source, target, sems.at[k]) for k, (source, target) in enumerate(pairs)]
    for copy in copies:
        copy.start()
    for copy in copies:
        copy.wait()


def first_kernel(seq_in, res_in, align_in, left_in, right_in, left_ref, right_ref, normed_ref, flat_ref, seq_ref, res_ref, align_ref, weight_ref, proj, sems):
    copied(
        [
            (align_in, align_ref),
            (left_in, weight_ref.at[0]),
            (right_in, weight_ref.at[1]),
            (seq_in, seq_ref),
            (res_in, res_ref),
        ],
        sems,
    )
    seqs, residues, width = align_ref.shape
    values = align_ref[...].reshape(seqs * residues, width)
    center = jnp.mean(values, axis=-1, keepdims=True)
    centred = values - center
    normed = centred * lax.rsqrt(jnp.mean(centred * centred, axis=-1, keepdims=True) + epsilon)
    flat_ref[...] = normed
    for s in range(seqs):
        normed_ref[:, s * width : (s + 1) * width] = normed[s * residues : (s + 1) * residues]
    weight = jnp.concatenate([weight_ref[0]] * 4 + [weight_ref[1]] * 4, axis=0)
    wide = lax.dot_general(normed, weight, (((1,), (1,)), ((), ())), precision=highest, preferred_element_type=f32)
    proj[0] = wide[:, :LANES]
    proj[1] = wide[:, LANES:]
    lane = lax.broadcasted_iota(jnp.int32, (seqs, LANES), 1)
    sub = lax.broadcasted_iota(jnp.int32, (seqs, LANES), 0)
    seq_live = jnp.zeros((seqs, LANES), f32)
    for s in range(seqs):
        seq_live = jnp.where(sub == s, seq_ref[s].astype(f32), seq_live)
    extra = jnp.where(lane == 64, seq_live, 0.0)
    group = lane // 32
    for quad in range(residues // 4):
        left = jnp.zeros((seqs, LANES), f32)
        right = jnp.zeros((seqs, LANES), f32)
        for g in range(4):
            i = quad * 4 + g
            live = res_ref[i].astype(f32)
            extra = jnp.where(lane == i, live, extra)
            here = group == g
            left = jnp.where(here, proj[0, pl.ds(i, seqs, stride=residues), :] * live, left)
            right = jnp.where(here, proj[1, pl.ds(i, seqs, stride=residues), :] * live, right)
        left_ref[:, quad * LANES : (quad + 1) * LANES] = left * seq_live
        right_ref[:, quad * LANES : (quad + 1) * LANES] = right * seq_live
    right_ref[:, residues * 32 :] = extra


def weights_kernel(outer_in, value_in, out_weight_in, mapped_ref, mixed_ref, out_ref, tall, value_ref, out_weight_ref, sems):
    copied([(outer_in, tall), (value_in, value_ref), (out_weight_in, out_weight_ref)], sems)
    for b in range(32):
        high, low = split_two(tall[pl.ds(b, 32, stride=32), :])
        mapped_ref[b * 32 : (b + 1) * 32, :LANES] = high
        mapped_ref[b * 32 : (b + 1) * 32, LANES:] = low
    heads = mixed_ref.shape[0]
    values = value_ref[...]
    entry = lax.broadcasted_iota(jnp.int32, (256, LANES), 0)
    group = lane_group((256, LANES), 32)
    within = lax.broadcasted_iota(jnp.int32, (256, LANES), 1) % 32
    for h in range(heads):
        pick = jnp.where(entry == h * 32 + within, 1.0, 0.0)
        tiled = jnp.dot(values, pick, precision=highest, preferred_element_type=f32)
        four = jnp.concatenate([tiled] * 4, axis=0)
        block = jnp.where(entry // 64 == group, four, 0.0)
        high, low = split_two(block)
        mixed_ref[h, :, :LANES] = high
        mixed_ref[h, :, LANES:] = low
    high, low = split_two(out_weight_ref[...].T)
    out_ref[0] = high
    out_ref[1] = low


def outer_rows(left, first_row, res_ref, right_two, mapped_ref, pair_ref, heads_two, seen, pair_out_ref, logits_ref, outer, high_ref, low_ref):
    cols = 48
    left_high, left_low = split_two(left)
    both = right_two[...]
    outer[...] = mxu(both, jnp.concatenate([left_high, left_high], axis=0)) + mxu(both[:, :LANES], left_low)
    for quad in range(ROWS_PER_STEP // 4):
        for four in range(8):
            parts = [
                outer[(four * 4 + v) * cols : (four * 4 + v + 1) * cols, quad * LANES : (quad + 1) * LANES]
                for v in range(4)
            ]
            for g, part in enumerate(swap_groups(parts)):
                high, low = split_two(part)
                at = (quad * 4 + g) * cols
                high_ref[at : at + cols, four * LANES : (four + 1) * LANES] = high
                low_ref[at : at + cols, four * LANES : (four + 1) * LANES] = low
    wide = mxu(high_ref[...], mapped_ref[...])
    sums = wide[:, :LANES] + wide[:, LANES:] + mxu(low_ref[...], mapped_ref[:, :LANES])
    pairs = []
    for i in range(ROWS_PER_STEP):
        live = res_ref[first_row + i].astype(f32)
        count = jnp.maximum(seen[0] * live, 1.0)
        pair = pair_ref[i] + sums[i * cols : (i + 1) * cols] / count
        pair_out_ref[i] = pair
        pairs.append(pair)
    pair = jnp.concatenate(pairs, axis=0)
    centred = pair - jnp.mean(pair, axis=-1, keepdims=True)
    normed = centred * lax.rsqrt(jnp.mean(centred * centred, axis=-1, keepdims=True) + epsilon)
    high, low = split_two(normed)
    normed_two = jnp.concatenate([high, low], axis=1)
    logits = mxu(normed_two, heads_two[0]) + mxu(normed_two, heads_two[1])
    lane = lax.broadcasted_iota(jnp.int32, (cols, LANES), 1)
    line = jnp.zeros((cols, LANES), f32)
    for i in range(ROWS_PER_STEP):
        line = jnp.where(lane // 8 == i, pltpu.roll(logits[i * cols : (i + 1) * cols], 8 * i, 1) if i else logits[:cols], line)
    logits_ref[...] = line + seen[1]


def outer_kernel(*refs):
    res_ref = refs[0]
    left_pieces = refs[1 : 1 + Z_CHIPS]
    right_pieces = refs[1 + Z_CHIPS : 9 + Z_CHIPS]
    mapped_ref, head_ref, pair_ref, pair_out_ref, logits_ref, right_two, seen, heads_two = refs[9 + Z_CHIPS : 17 + Z_CHIPS]
    left_all, right_ref, tall, outer, high_ref, low_ref = refs[17 + Z_CHIPS :]
    step = pl.program_id(0)
    cols = 48

    @pl.when(step == 0)
    def _():
        me = lax.axis_index("col")
        side, place = me // Z_CHIPS, lax.rem(me, Z_CHIPS)
        for k, piece in enumerate(left_pieces):
            at = lax.rem(place + k, Z_CHIPS)
            left_all[pl.ds(pl.multiple_of((side * Z_CHIPS + at) * 8, 8), 8), :] = piece[0]
            left_all[pl.ds(pl.multiple_of(((1 - side) * Z_CHIPS + at) * 8, 8), 8), :] = piece[1]
        row = lax.axis_index("row")
        x, y, core = row // 4, lax.rem(row // 2, 2), lax.rem(row, 2)
        for k, piece in enumerate(right_pieces):
            at = lax.rem(x + k % 4, 4) * 4 + (core if k < 4 else 1 - core)
            right_ref[pl.ds(pl.multiple_of((at + y * 2) * 8, 8), 8), :] = piece[0]
            right_ref[pl.ds(pl.multiple_of((at + (1 - y) * 2) * 8, 8), 8), :] = piece[1]
        tall[...] = right_ref[:, : cols * 32].T
        for b in range(32):
            high, low = split_two(tall[pl.ds(b, cols, stride=32), :])
            right_two[b * cols : (b + 1) * cols, :LANES] = high
            right_two[b * cols : (b + 1) * cols, LANES:] = low
        extra = right_ref[:, cols * 32 :]
        lane = lax.broadcasted_iota(jnp.int32, (LANES, LANES), 1)
        total = jnp.sum(jnp.where(lane == 64, extra, 0.0))
        live_cols = extra.T[:cols, :1]
        seen[0] = jnp.broadcast_to(live_cols * total, (cols, LANES))
        seen[1] = jnp.broadcast_to((live_cols - 1.0) * 1e9, (cols, LANES))
        head = jnp.concatenate([head_ref[...], jnp.zeros((LANES - head_ref.shape[0], LANES), f32)], axis=0).T
        head_high, head_low = split_two(head)
        heads_two[0, :LANES] = head_high
        heads_two[0, LANES:] = head_high
        heads_two[1, :LANES] = head_low
        heads_two[1, LANES:] = head_low

    left = left_all[:, pl.ds(pl.multiple_of(step * (ROWS_PER_STEP * 32), LANES), ROWS_PER_STEP * 32)]
    outer_rows(left, step * ROWS_PER_STEP, res_ref, right_two, mapped_ref, pair_ref, heads_two, seen, pair_out_ref, logits_ref, outer, high_ref, low_ref)


def middle_kernel(align_normed_ref, gate_ref, *refs):
    pieces = refs[:8]
    turned_high_ref, turned_low_ref, open_ref, held = refs[8:]
    residues = pieces[0].shape[1]
    row = lax.axis_index("row")
    x, y, core = row // 4, lax.rem(row // 2, 2), lax.rem(row, 2)
    for k, piece in enumerate(pieces):
        at = lax.rem(x + k % 4, 4) * 4 + (core if k < 4 else 1 - core)
        held[pl.ds(pl.multiple_of((at + y * 2) * residues, 8), residues), :] = piece[0]
        held[pl.ds(pl.multiple_of((at + (1 - y) * 2) * residues, 8), residues), :] = piece[1]
    high, low = split_two(held[...].T)
    turned_high_ref[...] = high
    turned_low_ref[...] = low
    wide = jnp.dot(align_normed_ref[...], gate_ref[...], precision=highest, preferred_element_type=f32)
    open_ref[...] = jax.nn.sigmoid(wide)


def last_kernel(*refs):
    pieces_in = refs[:Z_CHIPS]
    turned_high_ref, turned_low_ref, mixed_ref, open_ref, out_weight_ref, align_ref, out_ref, held, averaged = refs[Z_CHIPS:]
    heads = mixed_ref.shape[0]
    rows = 48
    me = lax.axis_index("col")
    side, place = me // Z_CHIPS, lax.rem(me, Z_CHIPS)
    for k, piece in enumerate(pieces_in):
        at = lax.rem(place + k, Z_CHIPS) * rows
        for other in range(2):
            half = side if other == 0 else 1 - side
            start = pl.multiple_of(half * (Z_CHIPS * rows) + at, 8)
            held[pl.ds(start, rows), :] = piece[other]
    logits = held[...]
    top = jnp.max(logits, axis=0, keepdims=True)
    expo = jnp.exp(logits - top)
    total = jnp.sum(expo, axis=0, keepdims=True)
    high, low = split_two(expo)
    turned_high = turned_high_ref[...]
    summed = mxu(turned_high, high) + mxu(turned_high, low) + mxu(turned_low_ref[...], high)
    turned = (summed / total).T
    for k in range(4):
        averaged[k] = turned[:, k * LANES : (k + 1) * LANES]
    ready = []
    for h in range(heads):
        one = [averaged[k, pl.ds(h, rows, stride=heads), :] for k in range(4)]
        one = jnp.concatenate([jnp.concatenate(one[:2], axis=1), jnp.concatenate(one[2:], axis=1)], axis=0)
        high, low = split_two(one)
        wide = mxu(high, mixed_ref[h])
        ready.append(wide[:, :LANES] + wide[:, LANES:] + mxu(low, mixed_ref[h, :, :LANES]))
    pieces = [[None, None] for _ in range(8)]
    for half in range(2):
        for s, part in enumerate(swap_groups(ready[half * 4 : half * 4 + 4])):
            pieces[s][half] = part[:rows]
            pieces[s + 4][half] = part[rows:]
    merged = jnp.concatenate([jnp.concatenate(p, axis=1) for p in pieces], axis=0)
    high, low = split_two(open_ref[...] * merged)
    result = mxu(high, out_weight_ref[0]) + mxu(high, out_weight_ref[1]) + mxu(low, out_weight_ref[0])
    out_ref[...] = align_ref[...] + result.reshape(out_ref.shape)


def row_pieces(shard, axis):
    devices = lax.axis_size(axis)
    both = jnp.stack([shard, lax.ppermute(shard, axis, [(d, d ^ 2) for d in range(devices)])])
    pieces = [both] + [
        lax.ppermute(both, axis, [(d, (d + devices - 4 * k) % devices) for d in range(devices)]) for k in (1, 2, 3)
    ]
    return pieces + [lax.ppermute(piece, axis, [(d, d ^ 1) for d in range(devices)]) for piece in pieces]


def ring_pieces(shard, axis, *first):
    devices = lax.axis_size(axis)
    ring = Z_CHIPS
    other = lax.ppermute(shard, axis, [(d, (d + ring) % devices) for d in range(devices)])
    both = after(jnp.stack([shard, other]), *first)

    def further(piece, k):
        return lax.ppermute(piece, axis, [(d, d // ring * ring + (d + ring - k) % ring) for d in range(devices)])

    pieces = {0: both}
    for k in (1, 7, 2, 6):
        pieces[k] = further(both, k)
    pieces[3] = further(pieces[2], 1)
    pieces[5] = further(pieces[6], 7)
    pieces[4] = further(pieces[2], 2)
    return [pieces[k] for k in range(ring)]


def in_hbm(array):
    return pltpu.with_memory_space_constraint(array, pltpu.HBM)


def after(value, *others):
    return lax.optimization_barrier((value, *others))[0]


def call(kernel, outs, limit, scratch=(), **more):
    return pl.pallas_call(
        kernel,
        out_shape=outs,
        scratch_shapes=list(scratch),
        compiler_params=pltpu.CompilerParams(vmem_limit_bytes=limit * 1024 * 1024),
        **more,
    )


def shape(dims, dtype=f32):
    return jax.ShapeDtypeStruct(dims, dtype)


VMEM = pl.BlockSpec(memory_space=pltpu.VMEM)
HBM = pl.BlockSpec(memory_space=pltpu.HBM)
SMEM = pl.BlockSpec(memory_space=pltpu.SMEM)


def per_device(n_row, n_col, alignment, pair_rep, seq_mask, res_mask, left_weight, right_weight, w_outer, w_logits, value_weight, gate_weight, output_weight):
    seqs, rows, width = alignment.shape
    cols = pair_rep.shape[1]
    pair_width = pair_rep.shape[2]
    left, right, normed, normed_flat = call(
        first_kernel,
        (shape((seqs, rows * 32)), shape((seqs, rows * 32 + LANES)), shape((rows, seqs * width)), shape((seqs * rows, width))),
        8,
        scratch=[
            pltpu.SMEM(seq_mask.shape, jnp.int32),
            pltpu.SMEM(res_mask.shape, jnp.int32),
            pltpu.VMEM(alignment.shape, f32),
            pltpu.VMEM((2, 32, width), f32),
            pltpu.VMEM((2, seqs * rows, LANES), f32),
            pltpu.SemaphoreType.DMA((5,)),
        ],
        in_specs=[HBM] * 5,
    )(*[in_hbm(a) for a in (seq_mask, res_mask, alignment, left_weight.T, right_weight.T)])
    turn = [(r * n_col + c, c * n_col + r) for r in range(n_row) for c in range(n_col)]
    right_here = lax.ppermute(right, ("row", "col"), turn)
    mapped, mixed, out_two = call(
        weights_kernel,
        (shape((1024, 256), bf16), shape((8, 256, 256), bf16), shape((2, 256, 64), bf16)),
        12,
        scratch=[
            pltpu.VMEM((1024, LANES), f32),
            pltpu.VMEM(value_weight.shape, f32),
            pltpu.VMEM((64, 256), f32),
            pltpu.SemaphoreType.DMA((3,)),
        ],
        in_specs=[HBM] * 3,
    )(*[in_hbm(a) for a in (w_outer, value_weight, output_weight.T)])
    left_pieces = ring_pieces(left, "col", mapped)
    right_pieces = row_pieces(right_here, "row")
    steps = rows // ROWS_PER_STEP
    pair_rep = in_hbm(pair_rep)
    pair_block = (ROWS_PER_STEP, cols, pair_width)
    work = [
        pltpu.VMEM((cols * 32, ROWS_PER_STEP * 32), f32),
        pltpu.VMEM((ROWS_PER_STEP * cols, 1024), bf16),
        pltpu.VMEM((ROWS_PER_STEP * cols, 1024), bf16),
    ]
    pair_out, logits = pl.pallas_call(
        outer_kernel,
        grid=(steps,),
        out_shape=(
            shape(pair_rep.shape),
            shape((cols, steps * LANES)),
        ),
        in_specs=[SMEM] + [VMEM] * 18 + [pl.BlockSpec(pair_block, lambda t: (t, 0, 0))],
        out_specs=[
            pl.BlockSpec(pair_block, lambda t: (t, 0, 0)),
            pl.BlockSpec((cols, LANES), lambda t: (0, t)),
        ],
        scratch_shapes=[
            pltpu.VMEM((cols * 32, 256), bf16),
            pltpu.VMEM((2, cols, LANES), f32),
            pltpu.VMEM((2, 256, LANES), bf16),
            pltpu.VMEM((n_col * seqs, rows * 32), f32),
            pltpu.VMEM((n_row * seqs, rows * 32 + LANES), f32),
            pltpu.VMEM((cols * 32, LANES), f32),
        ]
        + work,
        compiler_params=pltpu.CompilerParams(vmem_limit_bytes=32 * 1024 * 1024),
        cost_estimate=pl.CostEstimate(flops=10**10, bytes_accessed=10**7, transcendentals=0),
    )(res_mask, *left_pieces, *right_pieces, mapped, w_logits.T, pair_rep)
    normed_pieces = row_pieces(normed, "row")
    turned_high, turned_low, opened = call(
        middle_kernel,
        (shape((seqs * width, n_row * rows), bf16), shape((seqs * width, n_row * rows), bf16), shape((seqs * rows, gate_weight.shape[1]))),
        12,
        scratch=[pltpu.VMEM((n_row * rows, seqs * width), f32)],
    )(normed_flat, gate_weight, *normed_pieces)
    pieces = ring_pieces(logits, "col")
    alignment_out = call(
        last_kernel,
        shape(alignment.shape),
        24,
        scratch=[pltpu.VMEM((n_row * rows, steps * LANES), f32), pltpu.VMEM((4, steps * LANES, LANES), f32)],
    )(*pieces, turned_high, turned_low, mixed, opened, out_two, alignment)
    return alignment_out, pair_out


def solution(mesh):
    in_specs = (
        P("col", "row", None),
        P("row", "col", None),
        P("col"),
        P("row"),
        P(),
        P(),
        P(),
        P(),
        P(),
        P(),
        P(),
    )
    out_specs = (P("col", "row", None), P("row", "col", None))
    body = functools.partial(per_device, mesh.shape["row"], mesh.shape["col"])
    return jax.shard_map(body, mesh=mesh, in_specs=in_specs, out_specs=out_specs, check_vma=False)
```

```python
import functools

import jax
import jax.numpy as jnp
from jax import lax
from jax.experimental import pallas as pl
from jax.experimental.pallas import tpu as pltpu
from jax.sharding import PartitionSpec as P

epsilon = 1e-05
highest = lax.Precision.HIGHEST
f32 = jnp.float32
bf16 = jnp.bfloat16
LANES = 128
Z_CHIPS = 8
ROWS_PER_STEP = 16


def split_two(values):
    high = values.astype(bf16)
    low = (values - high.astype(f32)).astype(bf16)
    return high, low


def mxu(left, right):
    return jnp.dot(left, right, preferred_element_type=f32)


def lane_group(shape, width):
    return lax.broadcasted_iota(jnp.int32, shape, len(shape) - 1) // width


def swap_groups(parts):
    group = lane_group(parts[0].shape, 32)
    upper = group >= 2
    odd = (group % 2) == 1
    first = list(parts)
    for v in (0, 1):
        mixed = pltpu.roll(jnp.where(upper, parts[v], parts[v + 2]), 64, 1)
        first[v] = jnp.where(upper, mixed, parts[v])
        first[v + 2] = jnp.where(upper, parts[v + 2], mixed)
    second = list(first)
    for v in (0, 2):
        second[v] = jnp.where(odd, pltpu.roll(first[v + 1], 32, 1), first[v])
        second[v + 1] = jnp.where(odd, first[v + 1], pltpu.roll(first[v], 96, 1))
    return second


def copied(pairs, sems):
    copies = [pltpu.make_async_copy(source, target, sems.at[k]) for k, (source, target) in enumerate(pairs)]
    for copy in copies:
        copy.start()
    for copy in copies:
        copy.wait()


def first_kernel(seq_in, res_in, align_in, left_in, right_in, left_ref, right_ref, normed_ref, flat_ref, seq_ref, res_ref, align_ref, weight_ref, proj, sems):
    copied(
        [
            (align_in, align_ref),
            (left_in, weight_ref.at[0]),
            (right_in, weight_ref.at[1]),
            (seq_in, seq_ref),
            (res_in, res_ref),
        ],
        sems,
    )
    seqs, residues, width = align_ref.shape
    values = align_ref[...].reshape(seqs * residues, width)
    center = jnp.mean(values, axis=-1, keepdims=True)
    centred = values - center
    normed = centred * lax.rsqrt(jnp.mean(centred * centred, axis=-1, keepdims=True) + epsilon)
    flat_ref[...] = normed
    for s in range(seqs):
        normed_ref[:, s * width : (s + 1) * width] = normed[s * residues : (s + 1) * residues]
    weight = jnp.concatenate([weight_ref[0]] * 4 + [weight_ref[1]] * 4, axis=0)
    wide = lax.dot_general(normed, weight, (((1,), (1,)), ((), ())), precision=highest, preferred_element_type=f32)
    proj[0] = wide[:, :LANES]
    proj[1] = wide[:, LANES:]
    lane = lax.broadcasted_iota(jnp.int32, (seqs, LANES), 1)
    sub = lax.broadcasted_iota(jnp.int32, (seqs, LANES), 0)
    seq_live = jnp.zeros((seqs, LANES), f32)
    for s in range(seqs):
        seq_live = jnp.where(sub == s, seq_ref[s].astype(f32), seq_live)
    extra = jnp.where(lane == 64, seq_live, 0.0)
    group = lane // 32
    for quad in range(residues // 4):
        left = jnp.zeros((seqs, LANES), f32)
        right = jnp.zeros((seqs, LANES), f32)
        for g in range(4):
            i = quad * 4 + g
            live = res_ref[i].astype(f32)
            extra = jnp.where(lane == i, live, extra)
            here = group == g
            left = jnp.where(here, proj[0, pl.ds(i, seqs, stride=residues), :] * live, left)
            right = jnp.where(here, proj[1, pl.ds(i, seqs, stride=residues), :] * live, right)
        left_ref[:, quad * LANES : (quad + 1) * LANES] = left * seq_live
        right_ref[:, quad * LANES : (quad + 1) * LANES] = right * seq_live
    right_ref[:, residues * 32 :] = extra


def weights_kernel(outer_in, value_in, out_weight_in, mapped_ref, mixed_ref, out_ref, tall, value_ref, out_weight_ref, sems):
    copied([(outer_in, tall), (value_in, value_ref), (out_weight_in, out_weight_ref)], sems)
    for b in range(32):
        high, low = split_two(tall[pl.ds(b, 32, stride=32), :])
        mapped_ref[b * 32 : (b + 1) * 32, :LANES] = high
        mapped_ref[b * 32 : (b + 1) * 32, LANES:] = low
    heads = mixed_ref.shape[0]
    values = value_ref[...]
    entry = lax.broadcasted_iota(jnp.int32, (256, LANES), 0)
    group = lane_group((256, LANES), 32)
    within = lax.broadcasted_iota(jnp.int32, (256, LANES), 1) % 32
    for h in range(heads):
        pick = jnp.where(entry == h * 32 + within, 1.0, 0.0)
        tiled = jnp.dot(values, pick, precision=highest, preferred_element_type=f32)
        four = jnp.concatenate([tiled] * 4, axis=0)
        block = jnp.where(entry // 64 == group, four, 0.0)
        high, low = split_two(block)
        mixed_ref[h, :, :LANES] = high
        mixed_ref[h, :, LANES:] = low
    high, low = split_two(out_weight_ref[...].T)
    out_ref[0] = high
    out_ref[1] = low


def right_kernel(head_ref, *refs):
    right_pieces = refs[:4]
    right_two, seen, heads_two, right_ref, tall = refs[4:]
    cols = 48
    for piece, at in row_places(right_pieces):
        right_ref[pl.ds(pl.multiple_of(at * 8, 8), 8), :] = piece[...]
    tall[...] = right_ref[:, : cols * 32].T
    for b in range(32):
        high, low = split_two(tall[pl.ds(b, cols, stride=32), :])
        right_two[b * cols : (b + 1) * cols, :LANES] = high
        right_two[b * cols : (b + 1) * cols, LANES : 2 * LANES] = low
        right_two[b * cols : (b + 1) * cols, 2 * LANES :] = high
    extra = right_ref[:, cols * 32 :]
    lane = lax.broadcasted_iota(jnp.int32, (LANES, LANES), 1)
    total = jnp.sum(jnp.where(lane == 64, extra, 0.0))
    live_cols = extra.T[:cols, :1]
    seen[0] = jnp.broadcast_to(live_cols * total, (cols, LANES))
    seen[1] = jnp.broadcast_to((live_cols - 1.0) * 1e9, (cols, LANES))
    head = jnp.concatenate([head_ref[...], jnp.zeros((LANES - head_ref.shape[0], LANES), f32)], axis=0).T
    head_high, head_low = split_two(head)
    heads_two[0, :LANES] = head_high
    heads_two[0, LANES:] = head_high
    heads_two[1, :LANES] = head_low
    heads_two[1, LANES:] = head_low


def outer_rows(left, first_row, res_ref, right_two, mapped_ref, pair_ref, heads_two, seen, pair_out_ref, logits_ref, outer, halves_ref):
    cols = 48
    left_high, left_low = split_two(left)
    outer[...] = mxu(right_two[...], jnp.concatenate([left_high, left_high, left_low], axis=0))
    for quad in range(ROWS_PER_STEP // 4):
        for four in range(8):
            parts = [
                outer[(four * 4 + v) * cols : (four * 4 + v + 1) * cols, quad * LANES : (quad + 1) * LANES]
                for v in range(4)
            ]
            for g, part in enumerate(swap_groups(parts)):
                high, low = split_two(part)
                at = (quad * 4 + g) * cols
                halves_ref[at : at + cols, four * LANES : (four + 1) * LANES] = high
                halves_ref[at : at + cols, 1024 + four * LANES : 1024 + (four + 1) * LANES] = low
    wide = mxu(halves_ref[:, :1024], mapped_ref[...])
    sums = wide[:, :LANES] + wide[:, LANES:] + mxu(halves_ref[:, 1024:], mapped_ref[:, :LANES])
    pairs = []
    for i in range(ROWS_PER_STEP):
        live = res_ref[first_row + i].astype(f32)
        count = jnp.maximum(seen[0] * live, 1.0)
        pair = pair_ref[i] + sums[i * cols : (i + 1) * cols] / count
        pair_out_ref[i] = pair
        pairs.append(pair)
    pair = jnp.concatenate(pairs, axis=0)
    centred = pair - jnp.mean(pair, axis=-1, keepdims=True)
    normed = centred * lax.rsqrt(jnp.mean(centred * centred, axis=-1, keepdims=True) + epsilon)
    high, low = split_two(normed)
    normed_two = jnp.concatenate([high, low], axis=1)
    logits = mxu(normed_two, heads_two[0]) + mxu(normed_two, heads_two[1])
    lane = lax.broadcasted_iota(jnp.int32, (cols, LANES), 1)
    line = jnp.zeros((cols, LANES), f32)
    for i in range(ROWS_PER_STEP):
        line = jnp.where(lane // 8 == i, pltpu.roll(logits[i * cols : (i + 1) * cols], 8 * i, 1) if i else logits[:cols], line)
    logits_ref[...] = line + seen[1]


def outer_kernel(*refs):
    res_ref = refs[0]
    left_pieces = refs[1:3]
    right_two, seen, heads_two, mapped_ref, pair_ref, pair_out_ref, logits_ref, left_all, outer, halves_ref = refs[3:]
    step = pl.program_id(0)
    cols = 48

    @pl.when(step == 0)
    def _():
        for piece, at in col_places(left_pieces):
            left_all[pl.ds(pl.multiple_of(at * 8, 8), 8), :] = piece[...]

    left = left_all[:, pl.ds(pl.multiple_of(step * (ROWS_PER_STEP * 32), LANES), ROWS_PER_STEP * 32)]
    outer_rows(left, step * ROWS_PER_STEP, res_ref, right_two, mapped_ref, pair_ref, heads_two, seen, pair_out_ref, logits_ref, outer, halves_ref)


def middle_kernel(align_normed_ref, gate_ref, *refs):
    pieces = refs[:4]
    turned_high_ref, turned_low_ref, open_ref, held = refs[4:]
    residues = pieces[0].shape[2]
    for piece, at in row_places(pieces):
        held[pl.ds(pl.multiple_of(at * residues, 8), residues), :] = piece[...]
    high, low = split_two(held[...].T)
    turned_high_ref[...] = high
    turned_low_ref[...] = low
    wide = jnp.dot(align_normed_ref[...], gate_ref[...], precision=highest, preferred_element_type=f32)
    open_ref[...] = jax.nn.sigmoid(wide)


def last_kernel(*refs):
    pieces = refs[:8]
    turned_high_ref, turned_low_ref, mixed_ref, open_ref, out_weight_ref, align_ref, out_ref, held, averaged = refs[8:]
    heads = mixed_ref.shape[0]
    rows = 48
    for piece, at in col_places(pieces):
        held[pl.ds(pl.multiple_of(at * rows, 8), rows), :] = piece[...]
    logits = held[...]
    top = jnp.max(logits, axis=0, keepdims=True)
    expo = jnp.exp(logits - top)
    total = jnp.sum(expo, axis=0, keepdims=True)
    high, low = split_two(expo)
    turned_high = turned_high_ref[...]
    summed = mxu(turned_high, high) + mxu(turned_high, low) + mxu(turned_low_ref[...], high)
    turned = (summed / total).T
    for k in range(4):
        averaged[k] = turned[:, k * LANES : (k + 1) * LANES]
    ready = []
    for h in range(heads):
        one = [averaged[k, pl.ds(h, rows, stride=heads), :] for k in range(4)]
        one = jnp.concatenate([jnp.concatenate(one[:2], axis=1), jnp.concatenate(one[2:], axis=1)], axis=0)
        high, low = split_two(one)
        wide = mxu(high, mixed_ref[h])
        ready.append(wide[:, :LANES] + wide[:, LANES:] + mxu(low, mixed_ref[h, :, :LANES]))
    pieces = [[None, None] for _ in range(8)]
    for half in range(2):
        for s, part in enumerate(swap_groups(ready[half * 4 : half * 4 + 4])):
            pieces[s][half] = part[:rows]
            pieces[s + 4][half] = part[rows:]
    merged = jnp.concatenate([jnp.concatenate(p, axis=1) for p in pieces], axis=0)
    high, low = split_two(open_ref[...] * merged)
    result = mxu(high, out_weight_ref[0]) + mxu(high, out_weight_ref[1]) + mxu(low, out_weight_ref[0])
    out_ref[...] = align_ref[...] + result.reshape(out_ref.shape)


def way(row):
    return 1 - 2 * (row % 2)


def row_pieces(shard, n_row):
    def further(piece, k):
        return lax.ppermute(piece, "row", [(r, (r - 4 * k * way(r)) % n_row) for r in range(n_row)])

    both = jnp.stack([shard, lax.ppermute(shard, "row", [(r, r ^ 2) for r in range(n_row)])])
    even = jnp.stack([both, further(both, 2)])
    odd = further(even, 1)
    return [even, odd] + [lax.ppermute(piece, "row", [(r, r ^ 1) for r in range(n_row)]) for piece in (even, odd)]


def row_places(pieces):
    row = lax.axis_index("row")
    x, y, core = row // 4, lax.rem(row // 2, 2), lax.rem(row, 2)
    forward = 1 - 2 * core
    for n, piece in enumerate(pieces):
        for m in range(2):
            k = n % 2 + 2 * m
            at = lax.rem(x + 4 + forward * k, 4) * 4 + core if n < 2 else lax.rem(x + 4 - forward * k, 4) * 4 + 1 - core
            yield piece.at[m, 0], at + y * 2
            yield piece.at[m, 1], at + (1 - y) * 2


def col_places(pieces):
    me = lax.axis_index("col")
    side, place = me // Z_CHIPS, lax.rem(me, Z_CHIPS)
    forward = 1 - 2 * lax.rem(lax.axis_index("row"), 2)
    if len(pieces) == 2:
        views = [(k, piece.at[n]) for piece, places in zip(pieces, ((0, 4, 2, 6), (1, 5, 3, 7))) for n, k in enumerate(places)]
    else:
        views = list(enumerate(pieces))
    for k, view in views:
        at = lax.rem(place + Z_CHIPS + forward * k, Z_CHIPS)
        yield view.at[0], side * Z_CHIPS + at
        yield view.at[1], (1 - side) * Z_CHIPS + at


def fewer_pieces(shard, n_row, n_col, *first):
    ring = Z_CHIPS

    def further(piece, k):
        pairs = [
            (r * n_col + c, r * n_col + c // ring * ring + (c - k * way(r)) % ring)
            for r in range(n_row)
            for c in range(n_col)
        ]
        return lax.ppermute(piece, ("row", "col"), pairs)

    other = lax.ppermute(shard, "col", [(c, (c + ring) % n_col) for c in range(n_col)])
    both = jnp.stack([shard, other])
    two = after(jnp.stack([both, further(both, 4)]), *first)
    four = jnp.concatenate([two, further(two, 2)])
    return [four, further(four, 1)]


def ring_pieces(shard, n_row, n_col, *first):
    ring = Z_CHIPS
    other = lax.ppermute(shard, "col", [(c, (c + ring) % n_col) for c in range(n_col)])
    both = after(jnp.stack([shard, other]), *first)

    def further(piece, k):
        pairs = [
            (r * n_col + c, r * n_col + c // ring * ring + (c - k * way(r)) % ring)
            for r in range(n_row)
            for c in range(n_col)
        ]
        return lax.ppermute(piece, ("row", "col"), pairs)

    pieces = {0: both}
    for k in (1, 7, 2, 6):
        pieces[k] = further(both, k)
    pieces[3] = further(pieces[2], 1)
    pieces[5] = further(pieces[6], 7)
    pieces[4] = further(pieces[2], 2)
    return [pieces[k] for k in range(ring)]


def in_hbm(array):
    return pltpu.with_memory_space_constraint(array, pltpu.HBM)


def after(value, *others):
    return lax.optimization_barrier((value, *others))[0]


def call(kernel, outs, limit, scratch=(), **more):
    return pl.pallas_call(
        kernel,
        out_shape=outs,
        scratch_shapes=list(scratch),
        compiler_params=pltpu.CompilerParams(vmem_limit_bytes=limit * 1024 * 1024),
        **more,
    )


def shape(dims, dtype=f32):
    return jax.ShapeDtypeStruct(dims, dtype)


VMEM = pl.BlockSpec(memory_space=pltpu.VMEM)
HBM = pl.BlockSpec(memory_space=pltpu.HBM)
SMEM = pl.BlockSpec(memory_space=pltpu.SMEM)


def per_device(n_row, n_col, alignment, pair_rep, seq_mask, res_mask, left_weight, right_weight, w_outer, w_logits, value_weight, gate_weight, output_weight):
    seqs, rows, width = alignment.shape
    cols = pair_rep.shape[1]
    pair_width = pair_rep.shape[2]
    left, right, normed, normed_flat = call(
        first_kernel,
        (shape((seqs, rows * 32)), shape((seqs, rows * 32 + LANES)), shape((rows, seqs * width)), shape((seqs * rows, width))),
        8,
        scratch=[
            pltpu.SMEM(seq_mask.shape, jnp.int32),
            pltpu.SMEM(res_mask.shape, jnp.int32),
            pltpu.VMEM(alignment.shape, f32),
            pltpu.VMEM((2, 32, width), f32),
            pltpu.VMEM((2, seqs * rows, LANES), f32),
            pltpu.SemaphoreType.DMA((5,)),
        ],
        in_specs=[HBM] * 5,
    )(*[in_hbm(a) for a in (seq_mask, res_mask, alignment, left_weight.T, right_weight.T)])
    turn = [(r * n_col + c, c * n_col + r) for r in range(n_row) for c in range(n_col)]
    right_here = lax.ppermute(right, ("row", "col"), turn)
    mapped, mixed, out_two = call(
        weights_kernel,
        (shape((1024, 256), bf16), shape((8, 256, 256), bf16), shape((2, 256, 64), bf16)),
        12,
        scratch=[
            pltpu.VMEM((1024, LANES), f32),
            pltpu.VMEM(value_weight.shape, f32),
            pltpu.VMEM((64, 256), f32),
            pltpu.SemaphoreType.DMA((3,)),
        ],
        in_specs=[HBM] * 3,
    )(*[in_hbm(a) for a in (w_outer, value_weight, output_weight.T)])
    left_pieces = fewer_pieces(left, n_row, n_col, mapped)
    right_pieces = row_pieces(right_here, n_row)
    right_two, seen, heads_two = call(
        right_kernel,
        (shape((cols * 32, 3 * LANES), bf16), shape((2, cols, LANES)), shape((2, 256, LANES), bf16)),
        16,
        scratch=[pltpu.VMEM((n_row * seqs, rows * 32 + LANES), f32), pltpu.VMEM((cols * 32, LANES), f32)],
    )(w_logits.T, *right_pieces)
    steps = rows // ROWS_PER_STEP
    pair_rep = in_hbm(pair_rep)
    pair_block = (ROWS_PER_STEP, cols, pair_width)
    work = [
        pltpu.VMEM((cols * 32, ROWS_PER_STEP * 32), f32),
        pltpu.VMEM((ROWS_PER_STEP * cols, 2048), bf16),
    ]
    pair_out, logits = pl.pallas_call(
        outer_kernel,
        grid=(steps,),
        out_shape=(
            shape(pair_rep.shape),
            shape((cols, steps * LANES)),
        ),
        in_specs=[SMEM] + [VMEM] * 6 + [pl.BlockSpec(pair_block, lambda t: (t, 0, 0))],
        out_specs=[
            pl.BlockSpec(pair_block, lambda t: (t, 0, 0)),
            pl.BlockSpec((cols, LANES), lambda t: (0, t)),
        ],
        scratch_shapes=[
            pltpu.VMEM((n_col * seqs, rows * 32), f32),
        ]
        + work,
        compiler_params=pltpu.CompilerParams(vmem_limit_bytes=32 * 1024 * 1024),
        cost_estimate=pl.CostEstimate(flops=10**10, bytes_accessed=10**7, transcendentals=0),
    )(res_mask, *left_pieces, right_two, seen, heads_two, mapped, pair_rep)
    normed_pieces = row_pieces(normed, n_row)
    turned_high, turned_low, opened = call(
        middle_kernel,
        (shape((seqs * width, n_row * rows), bf16), shape((seqs * width, n_row * rows), bf16), shape((seqs * rows, gate_weight.shape[1]))),
        12,
        scratch=[pltpu.VMEM((n_row * rows, seqs * width), f32)],
    )(normed_flat, gate_weight, *normed_pieces)
    pieces = ring_pieces(logits, n_row, n_col)
    alignment_out = call(
        last_kernel,
        shape(alignment.shape),
        24,
        scratch=[pltpu.VMEM((n_row * rows, steps * LANES), f32), pltpu.VMEM((4, steps * LANES, LANES), f32)],
    )(*pieces, turned_high, turned_low, mixed, opened, out_two, alignment)
    return alignment_out, pair_out


def solution(mesh):
    in_specs = (
        P("col", "row", None),
        P("row", "col", None),
        P("col"),
        P("row"),
        P(),
        P(),
        P(),
        P(),
        P(),
        P(),
        P(),
    )
    out_specs = (P("col", "row", None), P("row", "col", None))
    body = functools.partial(per_device, mesh.shape["row"], mesh.shape["col"])
    return jax.shard_map(body, mesh=mesh, in_specs=in_specs, out_specs=out_specs, check_vma=False)
```

```python
import functools

import jax
import jax.numpy as jnp
from jax import lax
from jax.experimental import pallas as pl
from jax.experimental.pallas import tpu as pltpu
from jax.sharding import PartitionSpec as P

epsilon = 1e-05
highest = lax.Precision.HIGHEST
f32 = jnp.float32
bf16 = jnp.bfloat16
LANES = 128
Z_CHIPS = 8
ROWS_PER_STEP = 16


def split_two(values):
    high = values.astype(bf16)
    low = (values - high.astype(f32)).astype(bf16)
    return high, low


def mxu(left, right):
    return jnp.dot(left, right, preferred_element_type=f32)


def lane_group(shape, width):
    return lax.broadcasted_iota(jnp.int32, shape, len(shape) - 1) // width


def swap_groups(parts):
    group = lane_group(parts[0].shape, 32)
    upper = group >= 2
    odd = (group % 2) == 1
    first = list(parts)
    for v in (0, 1):
        mixed = pltpu.roll(jnp.where(upper, parts[v], parts[v + 2]), 64, 1)
        first[v] = jnp.where(upper, mixed, parts[v])
        first[v + 2] = jnp.where(upper, parts[v + 2], mixed)
    second = list(first)
    for v in (0, 2):
        second[v] = jnp.where(odd, pltpu.roll(first[v + 1], 32, 1), first[v])
        second[v + 1] = jnp.where(odd, first[v + 1], pltpu.roll(first[v], 96, 1))
    return second


def copied(pairs, sems):
    copies = [pltpu.make_async_copy(source, target, sems.at[k]) for k, (source, target) in enumerate(pairs)]
    for copy in copies:
        copy.start()
    for copy in copies:
        copy.wait()


def first_kernel(seq_in, res_in, align_in, left_in, right_in, left_ref, right_ref, normed_ref, flat_ref, seq_ref, res_ref, align_ref, weight_ref, proj, sems):
    copied(
        [
            (align_in, align_ref),
            (left_in, weight_ref.at[0]),
            (right_in, weight_ref.at[1]),
            (seq_in, seq_ref),
            (res_in, res_ref),
        ],
        sems,
    )
    seqs, residues, width = align_ref.shape
    values = align_ref[...].reshape(seqs * residues, width)
    center = jnp.mean(values, axis=-1, keepdims=True)
    centred = values - center
    normed = centred * lax.rsqrt(jnp.mean(centred * centred, axis=-1, keepdims=True) + epsilon)
    flat_ref[...] = normed
    for s in range(seqs):
        normed_ref[:, s * width : (s + 1) * width] = normed[s * residues : (s + 1) * residues]
    weight = jnp.concatenate([weight_ref[0]] * 4 + [weight_ref[1]] * 4, axis=0)
    wide = lax.dot_general(normed, weight, (((1,), (1,)), ((), ())), precision=highest, preferred_element_type=f32)
    proj[0] = wide[:, :LANES]
    proj[1] = wide[:, LANES:]
    lane = lax.broadcasted_iota(jnp.int32, (seqs, LANES), 1)
    sub = lax.broadcasted_iota(jnp.int32, (seqs, LANES), 0)
    seq_live = jnp.zeros((seqs, LANES), f32)
    for s in range(seqs):
        seq_live = jnp.where(sub == s, seq_ref[s].astype(f32), seq_live)
    extra = jnp.where(lane == 64, seq_live, 0.0)
    group = lane // 32
    for quad in range(residues // 4):
        left = jnp.zeros((seqs, LANES), f32)
        right = jnp.zeros((seqs, LANES), f32)
        for g in range(4):
            i = quad * 4 + g
            live = res_ref[i].astype(f32)
            extra = jnp.where(lane == i, live, extra)
            here = group == g
            left = jnp.where(here, proj[0, pl.ds(i, seqs, stride=residues), :] * live, left)
            right = jnp.where(here, proj[1, pl.ds(i, seqs, stride=residues), :] * live, right)
        left_ref[:, quad * LANES : (quad + 1) * LANES] = left * seq_live
        right_ref[:, quad * LANES : (quad + 1) * LANES] = right * seq_live
    right_ref[:, residues * 32 :] = extra


def weights_kernel(outer_in, value_in, out_weight_in, mapped_ref, mixed_ref, out_ref, tall, value_ref, out_weight_ref, sems):
    copied([(outer_in, tall), (value_in, value_ref), (out_weight_in, out_weight_ref)], sems)
    for b in range(32):
        high, low = split_two(tall[pl.ds(b, 32, stride=32), :])
        mapped_ref[b * 32 : (b + 1) * 32, :LANES] = high
        mapped_ref[b * 32 : (b + 1) * 32, LANES:] = low
    heads = mixed_ref.shape[0]
    values = value_ref[...]
    entry = lax.broadcasted_iota(jnp.int32, (256, LANES), 0)
    group = lane_group((256, LANES), 32)
    within = lax.broadcasted_iota(jnp.int32, (256, LANES), 1) % 32
    for h in range(heads):
        pick = jnp.where(entry == h * 32 + within, 1.0, 0.0)
        tiled = jnp.dot(values, pick, precision=highest, preferred_element_type=f32)
        four = jnp.concatenate([tiled] * 4, axis=0)
        block = jnp.where(entry // 64 == group, four, 0.0)
        high, low = split_two(block)
        mixed_ref[h, :, :LANES] = high
        mixed_ref[h, :, LANES:] = low
    high, low = split_two(out_weight_ref[...].T)
    out_ref[0] = high
    out_ref[1] = low


def right_kernel(head_ref, *refs):
    right_pieces = refs[:4]
    right_two, seen, heads_two, right_ref, tall = refs[4:]
    cols = 48
    for piece, at in row_places(right_pieces):
        right_ref[pl.ds(pl.multiple_of(at * 8, 8), 8), :] = piece[...]
    tall[...] = right_ref[:, : cols * 32].T
    for b in range(32):
        high, low = split_two(tall[pl.ds(b, cols, stride=32), :])
        right_two[b * cols : (b + 1) * cols, :LANES] = high
        right_two[b * cols : (b + 1) * cols, LANES : 2 * LANES] = low
        right_two[b * cols : (b + 1) * cols, 2 * LANES :] = high
    extra = right_ref[:, cols * 32 :]
    lane = lax.broadcasted_iota(jnp.int32, (LANES, LANES), 1)
    total = jnp.sum(jnp.where(lane == 64, extra, 0.0))
    live_cols = extra.T[:cols, :1]
    seen[0] = jnp.broadcast_to(live_cols * total, (cols, LANES))
    seen[1] = jnp.broadcast_to((live_cols - 1.0) * 1e9, (cols, LANES))
    head = jnp.concatenate([head_ref[...], jnp.zeros((LANES - head_ref.shape[0], LANES), f32)], axis=0).T
    head_high, head_low = split_two(head)
    heads_two[0, :LANES] = head_high
    heads_two[0, LANES:] = head_high
    heads_two[1, :LANES] = head_low
    heads_two[1, LANES:] = head_low


def outer_rows(left, first_row, res_ref, right_two, mapped_ref, pair_ref, heads_two, seen, pair_out_ref, logits_ref, outer, halves_ref):
    cols = 48
    left_high, left_low = split_two(left)
    outer[...] = mxu(right_two[...], jnp.concatenate([left_high, left_high, left_low], axis=0))
    for quad in range(ROWS_PER_STEP // 4):
        for four in range(8):
            parts = [
                outer[(four * 4 + v) * cols : (four * 4 + v + 1) * cols, quad * LANES : (quad + 1) * LANES]
                for v in range(4)
            ]
            for g, part in enumerate(swap_groups(parts)):
                high, low = split_two(part)
                at = (quad * 4 + g) * cols
                halves_ref[at : at + cols, four * LANES : (four + 1) * LANES] = high
                halves_ref[at : at + cols, 1024 + four * LANES : 1024 + (four + 1) * LANES] = low
    wide = mxu(halves_ref[:, :1024], mapped_ref[...])
    sums = wide[:, :LANES] + wide[:, LANES:] + mxu(halves_ref[:, 1024:], mapped_ref[:, :LANES])
    pairs = []
    for i in range(ROWS_PER_STEP):
        live = res_ref[first_row + i].astype(f32)
        count = jnp.maximum(seen[0] * live, 1.0)
        pair = pair_ref[i] + sums[i * cols : (i + 1) * cols] / count
        pair_out_ref[i] = pair
        pairs.append(pair)
    pair = jnp.concatenate(pairs, axis=0)
    centred = pair - jnp.mean(pair, axis=-1, keepdims=True)
    normed = centred * lax.rsqrt(jnp.mean(centred * centred, axis=-1, keepdims=True) + epsilon)
    high, low = split_two(normed)
    normed_two = jnp.concatenate([high, low], axis=1)
    logits = mxu(normed_two, heads_two[0]) + mxu(normed_two, heads_two[1])
    lane = lax.broadcasted_iota(jnp.int32, (cols, LANES), 1)
    line = jnp.zeros((cols, LANES), f32)
    for i in range(ROWS_PER_STEP):
        line = jnp.where(lane // 8 == i, pltpu.roll(logits[i * cols : (i + 1) * cols], 8 * i, 1) if i else logits[:cols], line)
    logits_ref[...] = line + seen[1]


def outer_kernel(*refs):
    res_ref = refs[0]
    left_pieces = refs[1:3]
    right_two, seen, heads_two, mapped_ref, pair_ref, pair_out_ref, logits_ref, left_all, outer, halves_ref = refs[3:]
    step = pl.program_id(0)
    cols = 48

    @pl.when(step == 0)
    def _():
        for piece, at in col_places(left_pieces):
            left_all[pl.ds(pl.multiple_of(at * 8, 8), 8), :] = piece[...]

    left = left_all[:, pl.ds(pl.multiple_of(step * (ROWS_PER_STEP * 32), LANES), ROWS_PER_STEP * 32)]
    outer_rows(left, step * ROWS_PER_STEP, res_ref, right_two, mapped_ref, pair_ref, heads_two, seen, pair_out_ref, logits_ref, outer, halves_ref)


def middle_kernel(align_normed_ref, gate_ref, *refs):
    pieces = refs[:4]
    turned_high_ref, turned_low_ref, open_ref, held = refs[4:]
    residues = pieces[0].shape[2]
    for piece, at in row_places(pieces):
        held[pl.ds(pl.multiple_of(at * residues, 8), residues), :] = piece[...]
    high, low = split_two(held[...].T)
    turned_high_ref[...] = high
    turned_low_ref[...] = low
    wide = jnp.dot(align_normed_ref[...], gate_ref[...], precision=highest, preferred_element_type=f32)
    open_ref[...] = jax.nn.sigmoid(wide)


def last_kernel(*refs):
    pieces = refs[:8]
    turned_high_ref, turned_low_ref, mixed_ref, open_ref, out_weight_ref, align_ref, out_ref, held, averaged = refs[8:]
    heads = mixed_ref.shape[0]
    rows = 48
    for piece, at in col_places(pieces):
        held[pl.ds(pl.multiple_of(at * rows, 8), rows), :] = piece[...]
    logits = held[...]
    top = jnp.max(logits, axis=0, keepdims=True)
    expo = jnp.exp(logits - top)
    total = jnp.sum(expo, axis=0, keepdims=True)
    high, low = split_two(expo)
    turned_high = turned_high_ref[...]
    summed = mxu(turned_high, high) + mxu(turned_high, low) + mxu(turned_low_ref[...], high)
    turned = (summed / total).T
    for k in range(4):
        averaged[k] = turned[:, k * LANES : (k + 1) * LANES]
    ready = []
    for h in range(heads):
        one = [averaged[k, pl.ds(h, rows, stride=heads), :] for k in range(4)]
        one = jnp.concatenate([jnp.concatenate(one[:2], axis=1), jnp.concatenate(one[2:], axis=1)], axis=0)
        high, low = split_two(one)
        wide = mxu(high, mixed_ref[h])
        ready.append(wide[:, :LANES] + wide[:, LANES:] + mxu(low, mixed_ref[h, :, :LANES]))
    pieces = [[None, None] for _ in range(8)]
    for half in range(2):
        for s, part in enumerate(swap_groups(ready[half * 4 : half * 4 + 4])):
            pieces[s][half] = part[:rows]
            pieces[s + 4][half] = part[rows:]
    merged = jnp.concatenate([jnp.concatenate(p, axis=1) for p in pieces], axis=0)
    high, low = split_two(open_ref[...] * merged)
    result = mxu(high, out_weight_ref[0]) + mxu(high, out_weight_ref[1]) + mxu(low, out_weight_ref[0])
    out_ref[...] = align_ref[...] + result.reshape(out_ref.shape)


def way(row):
    return 1 - 2 * (row % 2)


def row_pieces(shard, n_row, *first):
    def further(piece, k):
        return lax.ppermute(piece, "row", [(r, (r - 4 * k * way(r)) % n_row) for r in range(n_row)])

    both = after(jnp.stack([shard, lax.ppermute(shard, "row", [(r, r ^ 2) for r in range(n_row)])]), *first)
    even = jnp.stack([both, further(both, 2)])
    odd = further(even, 1)
    return [even, odd] + [lax.ppermute(piece, "row", [(r, r ^ 1) for r in range(n_row)]) for piece in (even, odd)]


def row_places(pieces):
    row = lax.axis_index("row")
    x, y, core = row // 4, lax.rem(row // 2, 2), lax.rem(row, 2)
    forward = 1 - 2 * core
    for n, piece in enumerate(pieces):
        for m in range(2):
            k = n % 2 + 2 * m
            at = lax.rem(x + 4 + forward * k, 4) * 4 + core if n < 2 else lax.rem(x + 4 - forward * k, 4) * 4 + 1 - core
            yield piece.at[m, 0], at + y * 2
            yield piece.at[m, 1], at + (1 - y) * 2


def col_places(pieces):
    me = lax.axis_index("col")
    side, place = me // Z_CHIPS, lax.rem(me, Z_CHIPS)
    forward = 1 - 2 * lax.rem(lax.axis_index("row"), 2)
    if len(pieces) == 2:
        views = [(k, piece.at[n]) for piece, places in zip(pieces, ((0, 4, 2, 6), (1, 5, 3, 7))) for n, k in enumerate(places)]
    else:
        views = list(enumerate(pieces))
    for k, view in views:
        at = lax.rem(place + Z_CHIPS + forward * k, Z_CHIPS)
        yield view.at[0], side * Z_CHIPS + at
        yield view.at[1], (1 - side) * Z_CHIPS + at


def fewer_pieces(shard, n_row, n_col, *first):
    ring = Z_CHIPS

    def further(piece, k):
        pairs = [
            (r * n_col + c, r * n_col + c // ring * ring + (c - k * way(r)) % ring)
            for r in range(n_row)
            for c in range(n_col)
        ]
        return lax.ppermute(piece, ("row", "col"), pairs)

    other = lax.ppermute(shard, "col", [(c, (c + ring) % n_col) for c in range(n_col)])
    both = jnp.stack([shard, other])
    two = after(jnp.stack([both, further(both, 4)]), *first)
    four = jnp.concatenate([two, further(two, 2)])
    return [four, further(four, 1)]


def ring_pieces(shard, n_row, n_col, *first):
    ring = Z_CHIPS
    other = lax.ppermute(shard, "col", [(c, (c + ring) % n_col) for c in range(n_col)])
    both = after(jnp.stack([shard, other]), *first)

    def further(piece, k):
        pairs = [
            (r * n_col + c, r * n_col + c // ring * ring + (c - k * way(r)) % ring)
            for r in range(n_row)
            for c in range(n_col)
        ]
        return lax.ppermute(piece, ("row", "col"), pairs)

    pieces = {0: both}
    for k in (1, 7, 2, 6):
        pieces[k] = further(both, k)
    pieces[3] = further(pieces[2], 1)
    pieces[5] = further(pieces[6], 7)
    pieces[4] = further(pieces[2], 2)
    return [pieces[k] for k in range(ring)]


def in_hbm(array):
    return pltpu.with_memory_space_constraint(array, pltpu.HBM)


def after(value, *others):
    return lax.optimization_barrier((value, *others))[0]


def call(kernel, outs, limit, scratch=(), **more):
    return pl.pallas_call(
        kernel,
        out_shape=outs,
        scratch_shapes=list(scratch),
        compiler_params=pltpu.CompilerParams(vmem_limit_bytes=limit * 1024 * 1024),
        **more,
    )


def shape(dims, dtype=f32):
    return jax.ShapeDtypeStruct(dims, dtype)


VMEM = pl.BlockSpec(memory_space=pltpu.VMEM)
HBM = pl.BlockSpec(memory_space=pltpu.HBM)
SMEM = pl.BlockSpec(memory_space=pltpu.SMEM)


def per_device(n_row, n_col, alignment, pair_rep, seq_mask, res_mask, left_weight, right_weight, w_outer, w_logits, value_weight, gate_weight, output_weight):
    seqs, rows, width = alignment.shape
    cols = pair_rep.shape[1]
    pair_width = pair_rep.shape[2]
    left, right, normed, normed_flat = call(
        first_kernel,
        (shape((seqs, rows * 32)), shape((seqs, rows * 32 + LANES)), shape((rows, seqs * width)), shape((seqs * rows, width))),
        8,
        scratch=[
            pltpu.SMEM(seq_mask.shape, jnp.int32),
            pltpu.SMEM(res_mask.shape, jnp.int32),
            pltpu.VMEM(alignment.shape, f32),
            pltpu.VMEM((2, 32, width), f32),
            pltpu.VMEM((2, seqs * rows, LANES), f32),
            pltpu.SemaphoreType.DMA((5,)),
        ],
        in_specs=[HBM] * 5,
    )(*[in_hbm(a) for a in (seq_mask, res_mask, alignment, left_weight.T, right_weight.T)])
    turn = [(r * n_col + c, c * n_col + r) for r in range(n_row) for c in range(n_col)]
    right_here = lax.ppermute(right, ("row", "col"), turn)
    mapped, mixed, out_two = call(
        weights_kernel,
        (shape((1024, 256), bf16), shape((8, 256, 256), bf16), shape((2, 256, 64), bf16)),
        12,
        scratch=[
            pltpu.VMEM((1024, LANES), f32),
            pltpu.VMEM(value_weight.shape, f32),
            pltpu.VMEM((64, 256), f32),
            pltpu.SemaphoreType.DMA((3,)),
        ],
        in_specs=[HBM] * 3,
    )(*[in_hbm(a) for a in (w_outer, value_weight, output_weight.T)])
    right_pieces = row_pieces(right_here, n_row, mapped)
    left_pieces = fewer_pieces(left, n_row, n_col)
    right_two, seen, heads_two = call(
        right_kernel,
        (shape((cols * 32, 3 * LANES), bf16), shape((2, cols, LANES)), shape((2, 256, LANES), bf16)),
        16,
        scratch=[pltpu.VMEM((n_row * seqs, rows * 32 + LANES), f32), pltpu.VMEM((cols * 32, LANES), f32)],
    )(w_logits.T, *right_pieces)
    steps = rows // ROWS_PER_STEP
    pair_rep = in_hbm(pair_rep)
    pair_block = (ROWS_PER_STEP, cols, pair_width)
    work = [
        pltpu.VMEM((cols * 32, ROWS_PER_STEP * 32), f32),
        pltpu.VMEM((ROWS_PER_STEP * cols, 2048), bf16),
    ]
    pair_out, logits = pl.pallas_call(
        outer_kernel,
        grid=(steps,),
        out_shape=(
            shape(pair_rep.shape),
            shape((cols, steps * LANES)),
        ),
        in_specs=[SMEM] + [VMEM] * 6 + [pl.BlockSpec(pair_block, lambda t: (t, 0, 0))],
        out_specs=[
            pl.BlockSpec(pair_block, lambda t: (t, 0, 0)),
            pl.BlockSpec((cols, LANES), lambda t: (0, t)),
        ],
        scratch_shapes=[
            pltpu.VMEM((n_col * seqs, rows * 32), f32),
        ]
        + work,
        compiler_params=pltpu.CompilerParams(vmem_limit_bytes=32 * 1024 * 1024),
        cost_estimate=pl.CostEstimate(flops=10**10, bytes_accessed=10**7, transcendentals=0),
    )(res_mask, *left_pieces, right_two, seen, heads_two, mapped, pair_rep)
    normed_pieces = row_pieces(normed, n_row)
    turned_high, turned_low, opened = call(
        middle_kernel,
        (shape((seqs * width, n_row * rows), bf16), shape((seqs * width, n_row * rows), bf16), shape((seqs * rows, gate_weight.shape[1]))),
        12,
        scratch=[pltpu.VMEM((n_row * rows, seqs * width), f32)],
    )(normed_flat, gate_weight, *normed_pieces)
    pieces = ring_pieces(logits, n_row, n_col)
    alignment_out = call(
        last_kernel,
        shape(alignment.shape),
        24,
        scratch=[pltpu.VMEM((n_row * rows, steps * LANES), f32), pltpu.VMEM((4, steps * LANES, LANES), f32)],
    )(*pieces, turned_high, turned_low, mixed, opened, out_two, alignment)
    return alignment_out, pair_out


def solution(mesh):
    in_specs = (
        P("col", "row", None),
        P("row", "col", None),
        P("col"),
        P("row"),
        P(),
        P(),
        P(),
        P(),
        P(),
        P(),
        P(),
    )
    out_specs = (P("col", "row", None), P("row", "col", None))
    body = functools.partial(per_device, mesh.shape["row"], mesh.shape["col"])
    return jax.shard_map(body, mesh=mesh, in_specs=in_specs, out_specs=out_specs, check_vma=False)
```
